32 devices in a mesh: dp: 4 (over y, x), ctx: 8 (over z, core).
Axes of the slice: x: 2, y: 2, z: 4, core: 2. Of those that a mesh axis runs over, the one named last changes fastest.
Arguments:
- query_rows: bfloat16 [4, 1024, 1024], P('dp', 'ctx'), may hold values from -0.59765625 to 0.59765625
- key_rows: bfloat16 [4, 1024, 1024], P('dp', 'ctx'), may hold values from -0.59765625 to 0.59765625
- value_rows: bfloat16 [4, 1024, 2048], P('dp', 'ctx'), may hold values from -6 to 6
- log_decay: bfloat16 [4, 1024, 1024], P('dp', 'ctx'), may hold values from -1 to 0, as said below
- out_grad: bfloat16 [4, 1024, 2048], P('dp', 'ctx'), may hold values from -1.796875 to 1.796875
- doc_ids: int32 [4, 1024], P('dp', 'ctx'), may hold values from 0 to 3, as said below
- block_order: int32 [4, 8, 4], P(None, 'ctx'), may hold values from 0 to 3, each once within a row
Outputs:
- attn_out: bfloat16 [4, 1024, 2048], P('dp', 'ctx')
- query_grad: bfloat16 [4, 1024, 1024], P('dp', 'ctx')
- key_grad: bfloat16 [4, 1024, 1024], P('dp', 'ctx')
- value_grad: bfloat16 [4, 1024, 2048], P('dp', 'ctx')
- decay_grad: bfloat16 [4, 1024, 1024], P('dp', 'ctx')
The draws below stay inside these ranges and needn't reach their ends.
Inputs may be any that keep to these rules, and one draw needn't show every extreme that they name: `log_decay`: nonpositive. `doc_ids`: never falls along a pack; every document number of a pack is used; each document has 1 to 512 positions, one of them exactly 512 and one 8 or fewer. `block_order`: each row of a device's list names each of its 4 blocks once.
All inputs are finite; a program needn't handle non-finite values.
Results may differ from the reference program's by a relative error of at most 0.0015.
Values may be sent and summed in bfloat16 or wider, within the bound.
A program may use at most 192 MiB of HBM per device.

```python
import jax
import jax.numpy as jnp
from jax import lax

HEADS = 16
DK = 64
DV = 128
TOK_DEV = 128
BLK = 32
DOCS = 4
PACKED_SEQUENCES = 4
PACK_POSITIONS = 1024
HK = 1024
HV = 2048
NB = 4
N_CTX = 8


def draw_log_decay(key, part):
    every_key = jax.random.split(key, 7)
    fast_share = 0.5
    fast_pick = jax.random.uniform(every_key[0], (HK,)) < fast_share
    fast_rate = jnp.exp(jax.random.uniform(every_key[1], (HK,), minval=jnp.log(0.02), maxval=jnp.log(0.05)))
    slow_rate = jnp.exp(jax.random.uniform(every_key[2], (HK,), minval=jnp.log(0.05 / PACK_POSITIONS), maxval=jnp.log(0.3 / PACK_POSITIONS)))
    every_rate = jnp.where(fast_pick, fast_rate, slow_rate)
    pieces_n = PACK_POSITIONS // TOK_DEV
    split_multiplier = jnp.exp(jax.random.uniform(every_key[3], (PACKED_SEQUENCES, pieces_n, 1, HK), minval=jnp.log(0.5), maxval=jnp.log(2.0)))
    split_multiplier = jnp.broadcast_to(split_multiplier, (PACKED_SEQUENCES, pieces_n, TOK_DEV, HK)).reshape(PACKED_SEQUENCES, PACK_POSITIONS, HK)
    random_offset = jax.random.uniform(every_key[4], (PACKED_SEQUENCES, PACK_POSITIONS, HK), minval=0.5, maxval=1.5)
    spike_position = (jax.random.uniform(every_key[5], (PACKED_SEQUENCES, PACK_POSITIONS, 1)) < 2.0 / PACK_POSITIONS).astype(jnp.float32)
    spike_length = jax.random.uniform(every_key[6], (PACKED_SEQUENCES, PACK_POSITIONS, 1), minval=0.2, maxval=0.5)
    gate_values = -(every_rate[None, None, :] * split_multiplier * random_offset) - spike_position * spike_length
    return gate_values.astype(jnp.float32).astype(jnp.bfloat16)


def draw_one_pack(pack_key):
    every_key = jax.random.split(pack_key, 3)
    half_len = PACK_POSITIONS // 2
    short_len = jax.random.randint(every_key[0], (), 1, 9).astype(jnp.int32)
    rest_len = (PACK_POSITIONS - half_len - short_len).astype(jnp.int32)
    third_len = jax.random.randint(every_key[1], (), 1, rest_len).astype(jnp.int32)
    lengths = jnp.stack([jnp.int32(half_len), short_len, third_len, rest_len - third_len]).astype(jnp.int32)
    order_pick = jax.random.permutation(every_key[2], DOCS)
    lengths = lengths[order_pick]
    ends = jnp.cumsum(lengths)[:DOCS - 1].astype(jnp.int32)
    positions = jnp.arange(PACK_POSITIONS, dtype=jnp.int32)
    return jnp.sum((positions[:, None] >= ends[None, :]).astype(jnp.int32), axis=1).astype(jnp.int32)


def draw_doc_ids(key, part):
    pack_keys = jax.random.split(jax.random.fold_in(key, 17), PACKED_SEQUENCES)
    return jax.vmap(draw_one_pack)(pack_keys).astype(jnp.int32)


def levels(own_key, dims, pieces, least, top_value):
    gain = 1.0
    for position, blocks in pieces:
        draws = jax.random.uniform(jax.random.fold_in(jax.random.fold_in(own_key, 6), position), (blocks,), jnp.float32, least / len(pieces), top_value / len(pieces))
        gain = gain * jnp.repeat(jnp.exp(draws), dims[position] // blocks).reshape((-1,) + (1,) * (len(dims) - 1 - position))
    return gain


def gaussian(own_key, shape, width, limit, cuts=(), kind=jnp.bfloat16):
    values = width * jax.random.normal(own_key, shape, jnp.float32)
    if cuts:
        values = values * levels(own_key, shape, cuts, -0.22, 0.18)
    return jnp.clip(values, -limit, limit).astype(kind)


def setup_inputs(seed: int = 0) -> dict:
    streams_of = jax.random.split(jax.random.key(seed), 8)
    query_rows = gaussian(streams_of[0], (PACKED_SEQUENCES, PACK_POSITIONS, HK), 0.1, 0.59765625, ((0, 4), (1, 8)))
    key_rows = gaussian(streams_of[1], (PACKED_SEQUENCES, PACK_POSITIONS, HK), 0.1, 0.59765625, ((0, 4), (1, 8)))
    value_rows = gaussian(streams_of[2], (PACKED_SEQUENCES, PACK_POSITIONS, HV), 1.0, 6.0, ((0, 4), (1, 8)))
    log_decay = draw_log_decay(jax.random.fold_in(streams_of[7], 71), 0)
    out_grad = gaussian(streams_of[4], (PACKED_SEQUENCES, PACK_POSITIONS, HV), 0.3, 1.796875, ((0, 4), (1, 8)))
    doc_ids = draw_doc_ids(jax.random.fold_in(streams_of[7], 71), 0)
    block_order = jax.vmap(lambda own: jax.random.permutation(own, NB))(jax.random.split(streams_of[6], PACKED_SEQUENCES * N_CTX)).reshape((PACKED_SEQUENCES, N_CTX, NB)).astype(jnp.int32)
    return {"query_rows": query_rows, "key_rows": key_rows, "value_rows": value_rows, "log_decay": log_decay, "out_grad": out_grad, "doc_ids": doc_ids, "block_order": block_order}


HIGH = lax.Precision.HIGHEST

def prepare(query_b, key_b, value_b, decay_b, doc_row):
    row_count = query_b.shape[0]
    head_count = query_b.shape[1] // DK
    query_f = query_b.astype(jnp.float32).reshape(row_count, head_count, DK)
    key_f = key_b.astype(jnp.float32).reshape(row_count, head_count, DK)
    value_f = value_b.astype(jnp.float32).reshape(row_count, head_count, DV)
    cumul = jnp.cumsum(decay_b.astype(jnp.float32).reshape(row_count, head_count, DK), axis=0)
    total_log = cumul[-1]
    growth = jnp.exp(cumul)
    shrink = jnp.exp(-cumul)
    to_end = jnp.exp(total_log[None] - cumul)
    later_pos = lax.broadcasted_iota(jnp.int32, (row_count, row_count), 0)
    earlier_pos = lax.broadcasted_iota(jnp.int32, (row_count, row_count), 1)
    same_doc = ((later_pos >= earlier_pos) & (doc_row[:, None] == doc_row[None, :])).astype(jnp.float32)
    first_id = doc_row[0]
    last_id = doc_row[-1]
    in_first = (doc_row == first_id).astype(jnp.float32)[:, None, None]
    in_last = (doc_row == last_id).astype(jnp.float32)[:, None, None]
    query_t = query_f * growth
    key_t = key_f * shrink
    scores = jnp.einsum('thi,shi->hts', query_t, key_t, precision=HIGH) * same_doc[None]
    return {'query_f': query_f, 'key_f': key_f, 'value_f': value_f, 'growth': growth, 'shrink': shrink, 'to_end': to_end, 'same_doc': same_doc, 'first_id': first_id, 'last_id': last_id, 'in_first': in_first, 'in_last': in_last, 'query_t': query_t, 'key_t': key_t, 'scores': scores, 'decay_all': jnp.exp(total_log)}

def state_end(parts):
    return jnp.einsum('shi,shj->hij', parts['key_f'] * parts['to_end'] * parts['in_last'], parts['value_f'], precision=HIGH)

def start_grad(parts, grad_f):
    factor = DK ** (-0.5)
    return factor * jnp.einsum('thi,thj->hij', parts['query_t'] * parts['in_first'], grad_f, precision=HIGH)

def finish(parts, grad_f, state_in, use_state, carry_in, use_carry):
    factor = DK ** (-0.5)
    head_w = parts['in_first'] * use_state
    tail_w = parts['in_last'] * use_carry
    attn_rows = factor * (jnp.einsum('hts,shj->thj', parts['scores'], parts['value_f'], precision=HIGH) + jnp.einsum('thi,hij->thj', parts['query_t'], state_in, precision=HIGH) * head_w)
    grad_scores = jnp.einsum('thj,shj->hts', grad_f, parts['value_f'], precision=HIGH) * parts['same_doc'][None]
    grad_query = factor * parts['growth'] * (jnp.einsum('hts,shi->thi', grad_scores, parts['key_t'], precision=HIGH) + jnp.einsum('thj,hij->thi', grad_f, state_in, precision=HIGH) * head_w)
    grad_value = factor * jnp.einsum('hts,thj->shj', parts['scores'], grad_f, precision=HIGH) + jnp.einsum('shi,hij->shj', parts['key_f'] * parts['to_end'], carry_in, precision=HIGH) * tail_w
    grad_key = factor * parts['shrink'] * jnp.einsum('hts,thi->shi', grad_scores, parts['query_t'], precision=HIGH) + parts['to_end'] * jnp.einsum('hij,shj->shi', carry_in, parts['value_f'], precision=HIGH) * tail_w
    grad_log = parts['query_f'] * grad_query - parts['key_f'] * grad_key
    sum_start = lax.optimization_barrier(jnp.sum(grad_log * parts['in_first'], axis=0))
    return (attn_rows, grad_query, grad_key, grad_value, grad_log, sum_start)

def decay_grad_of(parts, grad_log, sums_in, use_carry):
    inside = jnp.einsum('ts,thi->shi', parts['same_doc'], grad_log, precision=HIGH)
    return inside + sums_in[None] * parts['in_last'] * use_carry

def move_in(raw_array, inverse):
    packs_n, seq_len, chans = raw_array.shape
    pieces_n = inverse.shape[1]
    block_n = inverse.shape[2]
    per_peer = block_n // packs_n
    blocks_all = raw_array.reshape(packs_n, pieces_n, block_n, BLK, chans)
    index_all = jnp.broadcast_to(inverse[:, :, :, None, None], blocks_all.shape)
    sent = jnp.take_along_axis(blocks_all, index_all, axis=2)
    sent = sent.reshape(packs_n, pieces_n, packs_n, per_peer, BLK, chans)
    return jnp.transpose(sent, (2, 1, 0, 3, 4, 5)).reshape(packs_n, seq_len, chans)

def move_out(balanced, order_all):
    packs_n, seq_len, chans = balanced.shape
    pieces_n = order_all.shape[1]
    block_n = order_all.shape[2]
    per_peer = block_n // packs_n
    parted = balanced.reshape(packs_n, pieces_n, packs_n, per_peer, BLK, chans)
    parted = jnp.transpose(parted, (2, 1, 0, 3, 4, 5)).reshape(packs_n, pieces_n, block_n, BLK, chans)
    index_all = jnp.broadcast_to(order_all[:, :, :, None, None], parted.shape)
    return jnp.take_along_axis(parted, index_all, axis=2).reshape(packs_n, seq_len, chans)

def one_pack(pack_in):
    query_p, key_p, value_p, decay_p, grad_p, doc_p = pack_in
    pieces_n = PACK_POSITIONS // TOK_DEV
    query_c = query_p.reshape(pieces_n, TOK_DEV, HK)
    key_c = key_p.reshape(pieces_n, TOK_DEV, HK)
    value_c = value_p.reshape(pieces_n, TOK_DEV, HV)
    decay_c = decay_p.reshape(pieces_n, TOK_DEV, HK)
    grad_c = grad_p.reshape(pieces_n, TOK_DEV, HV)
    doc_c = doc_p.reshape(pieces_n, TOK_DEV)

    def forward_step(carried, piece_in):
        state_in, prior_last = carried
        parts = prepare(*piece_in)
        use_state = (prior_last == parts['first_id']).astype(jnp.float32)
        single = (parts['first_id'] == parts['last_id']).astype(jnp.float32)
        state_out = state_end(parts) + single * use_state * parts['decay_all'][..., None] * state_in
        return ((state_out, parts['last_id']), (state_in, use_state))
    start = (jnp.zeros((HEADS, DK, DV), jnp.float32), jnp.int32(-1))
    unused_end, (states_in, uses_in) = lax.scan(forward_step, start, (query_c, key_c, value_c, decay_c, doc_c))

    def reverse_step(carried, piece_in):
        carry_in, sums_in, next_first = carried
        query_b, key_b, value_b, decay_b, doc_row, grad_b, state_in, use_state = piece_in
        parts = prepare(query_b, key_b, value_b, decay_b, doc_row)
        grad_f = grad_b.astype(jnp.float32).reshape(TOK_DEV, HEADS, DV)
        use_carry = (next_first == parts['last_id']).astype(jnp.float32)
        single = (parts['first_id'] == parts['last_id']).astype(jnp.float32)
        attn_rows, grad_query, grad_key, grad_value, grad_log, sum_start = finish(parts, grad_f, state_in, use_state, carry_in, use_carry)
        grad_decay = decay_grad_of(parts, grad_log, sums_in, use_carry)
        carry_out = start_grad(parts, grad_f) + single * use_carry * parts['decay_all'][..., None] * carry_in
        sums_out = sum_start + single * use_carry * sums_in
        results = (attn_rows.reshape(TOK_DEV, HV), grad_query.reshape(TOK_DEV, HK), grad_key.reshape(TOK_DEV, HK), grad_value.reshape(TOK_DEV, HV), grad_decay.reshape(TOK_DEV, HK))
        return ((carry_out, sums_out, parts['first_id']), results)
    start_back = (jnp.zeros((HEADS, DK, DV), jnp.float32), jnp.zeros((HEADS, DK), jnp.float32), jnp.int32(-1))
    unused_back, results = lax.scan(reverse_step, start_back, (query_c, key_c, value_c, decay_c, doc_c, grad_c, states_in, uses_in), reverse=True)
    return tuple((item.reshape(PACK_POSITIONS, item.shape[-1]) for item in results))

def reference(query_rows, key_rows, value_rows, log_decay, out_grad, doc_ids, block_order):
    inverse = jnp.argsort(block_order, axis=2).astype(jnp.int32)
    query_bal = move_in(query_rows, inverse)
    key_bal = move_in(key_rows, inverse)
    value_bal = move_in(value_rows, inverse)
    decay_bal = move_in(log_decay, inverse)
    attn_all, query_all, key_all, value_all, decay_all = lax.map(one_pack, (query_bal, key_bal, value_bal, decay_bal, out_grad, doc_ids))
    attn_out = attn_all.astype(jnp.bfloat16)
    query_grad = move_out(query_all.astype(jnp.bfloat16), block_order)
    key_grad = move_out(key_all.astype(jnp.bfloat16), block_order)
    value_grad = move_out(value_all.astype(jnp.bfloat16), block_order)
    decay_grad = move_out(decay_all.astype(jnp.bfloat16), block_order)
    return (attn_out, query_grad, key_grad, value_grad, decay_grad)
```

```python
import functools

import jax
import jax.numpy as jnp
from jax import lax
from jax.experimental import pallas as pl
from jax.experimental.pallas import tpu as pltpu
from jax.sharding import PartitionSpec as P

DK = 64
DV = 128
BLK = 32
KW = 2 * DK
VW = 2 * DV
W = 3 * KW + VW
MESH = pl.DeviceIdType.MESH
F32 = jnp.float32
BF16 = jnp.bfloat16

NN = (((1,), (0,)), ((), ()))
NT = (((1,), (1,)), ((), ()))
TN = (((0,), (0,)), ((), ()))


def split(x):
    hi = x.astype(BF16)
    return hi, (x - hi.astype(F32)).astype(BF16)


def dot(a, b, dims):
    a = a if isinstance(a, tuple) else (a,)
    b = b if isinstance(b, tuple) else (b,)
    total = None
    for i, left in enumerate(a):
        for j, right in enumerate(b):
            if i + j > 1:
                continue
            term = lax.dot_general(left, right, dims, preferred_element_type=F32)
            total = term if total is None else total + term
    return total


def both(fn, pair):
    return tuple(fn(x) for x in pair)


def kernel(
    n_dp, n_ctx, order_hbm, doc_hbm, q_hbm, k_hbm, v_hbm, d_hbm, g_hbm,
    out_ref, ry,
    order_ref, doc_ref, q_ref, k_ref, v_ref, d_ref, g_ref, in_sem, decay, grow, end, near, dv_near, dq_near, dk_near,
    sx, rx, sy, loc, into, mate_out, mate_in, chain_out, chain_in, doc_prev, doc_next,
    x_send, x_recv, y_send, y_recv, mate_send, mate_recv, chain_send, chain_recv, far_send, far_recv, doc_send, doc_recv,
):
    me = lax.axis_index("dp")
    pos = lax.axis_index("ctx")
    rows = q_hbm.shape[1]
    pairs = q_hbm.shape[2] // KW
    blocks = rows // BLK
    per = blocks // n_dp
    part = per * BLK
    chips = n_ctx // 2
    has_prev = pos > 0
    has_next = pos < n_ctx - 1
    core = lax.rem(pos, 2)
    own = 1 - core
    mate_pos = pos + 1 - 2 * core
    ahead = 4 * core - 2
    chip = pos // 2
    hops = jnp.where(core == 1, chip, chips - 1 - chip)
    has_from = hops > 0
    has_to = hops < chips - 1

    barrier = pltpu.get_barrier_semaphore()
    for r in range(1, n_dp):
        peer = lax.rem(me + r, n_dp)
        pl.semaphore_signal(barrier, inc=1, device_id={"dp": peer}, device_id_type=MESH)

    peers = n_dp - 1
    for step in (-2, -1, 1, 2):
        there = (pos + step >= 0) & (pos + step < n_ctx)
        peers = peers + there.astype(jnp.int32)

        @pl.when(there)
        def _():
            pl.semaphore_signal(barrier, inc=1, device_id={"ctx": pos + step}, device_id_type=MESH)

    fetches = [
        pltpu.make_async_copy(src, dst, in_sem.at[i])
        for i, (src, dst) in enumerate((
            (order_hbm, order_ref), (q_hbm, q_ref), (k_hbm, k_ref), (d_hbm, d_ref),
            (v_hbm, v_ref), (doc_hbm, doc_ref), (g_hbm, g_ref),
        ))
    ]
    for fetch in fetches:
        fetch.start()

    def my_rows(index):
        return pl.ds(pl.multiple_of(index * part, part), part)

    def lanes(h, width):
        return pl.ds(pl.multiple_of(h * width, width), width)

    for fetch in fetches[:5]:
        fetch.wait()

    @pl.when(jnp.logical_not(has_prev))
    def _():
        doc_prev[...] = jnp.full_like(doc_prev, -1)

    @pl.when(jnp.logical_not(has_next))
    def _():
        doc_next[...] = jnp.full_like(doc_next, -1)

    @pl.when(jnp.logical_not(has_from))
    def _():
        chain_in[...] = jnp.zeros_like(chain_in)

    pl.semaphore_wait(barrier, peers)

    def exchange(src, dst, send, recv, h, r):
        peer = lax.rem(me + r, n_dp)
        return pltpu.make_async_remote_copy(
            src_ref=src.at[h, my_rows(peer), :],
            dst_ref=dst.at[h, my_rows(me), :],
            send_sem=send.at[h, r],
            recv_sem=recv.at[h, r],
            device_id={"dp": peer},
            device_id_type=MESH,
        )

    def arrival(src, dst, send, recv, h, r):
        source = lax.rem(me + n_dp - r, n_dp)
        return pltpu.make_async_remote_copy(
            src_ref=src.at[h, my_rows(source), :],
            dst_ref=dst.at[h, my_rows(source), :],
            send_sem=send.at[h, r],
            recv_sem=recv.at[h, r],
            device_id={"dp": source},
            device_id_type=MESH,
        )

    def to_ctx(src, dst, send, recv, there):
        return pltpu.make_async_remote_copy(
            src_ref=src, dst_ref=dst, send_sem=send, recv_sem=recv,
            device_id={"ctx": there}, device_id_type=MESH,
        )

    def doc_up():
        return to_ctx(doc_ref, doc_prev, doc_send.at[0], doc_recv.at[0], pos + 1)

    def doc_down():
        return to_ctx(doc_ref, doc_next, doc_send.at[1], doc_recv.at[1], pos - 1)

    def mate(h):
        return to_ctx(mate_out.at[h], mate_in.at[h], mate_send.at[h], mate_recv.at[h], mate_pos)

    def chain(h):
        return to_ctx(chain_out.at[h], chain_in.at[h], chain_send.at[h], chain_recv.at[h], pos + ahead)

    def far(h):
        return to_ctx(chain_in.at[h], into.at[own, h], far_send.at[h], far_recv.at[h], mate_pos)

    def far_arrival(h):
        return to_ctx(chain_in.at[h], into.at[1 - own, h], far_send.at[h], far_recv.at[h], mate_pos)

    order = [order_ref[me, 0, j] for j in range(blocks)]

    def piece(j):
        return slice(j * BLK, (j + 1) * BLK)

    def stage(h, carry):
        for src, width, at in ((q_ref, KW, 0), (k_ref, KW, KW), (d_ref, KW, 2 * KW), (v_ref, VW, 3 * KW)):
            parts = [src[0, piece(j), lanes(h, width)] for j in range(blocks)]
            for dest in range(blocks):
                chosen = parts[0]
                for j in range(1, blocks):
                    chosen = lax.select(order[j] == dest, parts[j], chosen)
                sx[h, piece(dest), at : at + width] = chosen
        rx[h, my_rows(me), :] = sx[h, my_rows(me), :]
        for r in range(1, n_dp):
            exchange(sx, rx, x_send, x_recv, h, r).start()
        return carry

    lax.fori_loop(0, pairs, stage, 0)

    for fetch in fetches[5:]:
        fetch.wait()

    @pl.when(has_next)
    def _():
        doc_up().start()

    @pl.when(has_prev)
    def _():
        doc_down().start()

    @pl.when(has_prev)
    def _():
        doc_up().wait_recv()

    @pl.when(has_next)
    def _():
        doc_down().wait_recv()

    doc_row = jnp.broadcast_to(doc_ref[...].astype(F32), (rows, rows))
    doc_col = doc_row.T
    first_row = doc_col[0:1, :]
    last_row = doc_col[rows - 1 : rows, :]
    prev_last = jnp.broadcast_to(doc_prev[:, rows - 1 : rows].astype(F32), (1, rows))
    next_first = jnp.broadcast_to(doc_next[:, 0:1].astype(F32), (1, rows))
    use_state = (prev_last == first_row).astype(F32)
    use_carry = (next_first == last_row).astype(F32)
    single = (first_row == last_row).astype(F32)
    pass_state = single * use_state
    pass_carry = single * use_carry
    pass_own = jnp.where(core == 1, pass_state, pass_carry)
    pass_mate = jnp.where(core == 1, pass_carry, pass_state)
    in_first = (doc_col == first_row).astype(F32)
    in_last = (doc_col == last_row).astype(F32)
    head_w = in_first * use_state
    tail_w = in_last * use_carry
    row_id = lax.broadcasted_iota(jnp.int32, (rows, rows), 0)
    lane_id = lax.broadcasted_iota(jnp.int32, (rows, rows), 1)
    same = (doc_row == doc_col) & (row_id >= lane_id)
    later = ((doc_row == doc_col) & (row_id <= lane_id)).astype(BF16)
    lower = (row_id >= lane_id).astype(BF16)
    in_a = lax.broadcasted_iota(jnp.int32, (rows, KW), 1) < DK
    factor = DK ** (-0.5)

    def load(h):
        q = rx[h, :, 0:KW]
        k = rx[h, :, KW : 2 * KW]
        d = rx[h, :, 2 * KW : 3 * KW]
        v = rx[h, :, 3 * KW : W]
        g = g_ref[0, :, lanes(h, VW)]
        cum = dot(lower, d, NN)
        total = cum[rows - 1 : rows, :]
        growth = jnp.exp(cum)
        shrink = jnp.exp(-cum)
        to_end = jnp.exp(total - cum)
        grow[h] = growth
        end[h] = to_end
        return q.astype(F32), k.astype(F32), v, g, d, growth, shrink, to_end

    def fold(wide):
        return jnp.concatenate([wide[0:DK, 0:DV], wide[DK:KW, DV:VW]], axis=0)

    def spread(tall):
        nil = jnp.zeros((DK, DV), tall.dtype)
        top = jnp.concatenate([tall[0:DK], nil], axis=1)
        low = jnp.concatenate([nil, tall[DK:KW]], axis=1)
        return jnp.concatenate([top, low], axis=0)

    def nearby(h):
        for r in range(1, n_dp):
            arrival(sx, rx, x_send, x_recv, h, r).wait_recv()
        q_f, k_f, v, g, d, growth, shrink, to_end = load(h)
        loc[0, h] = fold(dot(split(k_f * to_end * in_last), v, TN))
        loc[1, h] = factor * fold(dot(split(q_f * growth * in_first), g, TN))
        decay[h] = jnp.exp(dot(d, jnp.ones((rows, DV), BF16), TN))
        mate_out[h, 0] = loc[1 - own, h]
        mate_out[h, 1] = pass_mate * decay[h]
        mate(h).start()
        q_t = q_f * growth
        k_t = k_f * shrink
        zero = jnp.zeros_like(q_t)
        q_2 = split(jnp.concatenate([jnp.where(in_a, q_t, zero), jnp.where(in_a, zero, q_t)], axis=0))
        k_s = split(k_t)
        k_2 = split(jnp.concatenate([jnp.where(in_a, k_t, zero), jnp.where(in_a, zero, k_t)], axis=0))
        same_2 = jnp.concatenate([same, same], axis=0)
        score_2 = split(jnp.where(same_2, dot(q_2, k_s, NT), 0.0))
        v_a, v_b = v[:, 0:DV], v[:, DV:VW]
        g_a, g_b = g[:, 0:DV], g[:, DV:VW]
        score_a = both(lambda x: x[0:rows], score_2)
        score_b = both(lambda x: x[rows : 2 * rows], score_2)
        near[h, :, 0:DV] = dot(score_a, v_a, NN)
        near[h, :, DV:VW] = dot(score_b, v_b, NN)
        dv_near[h, :, 0:DV] = dot(score_a, g_a, TN)
        dv_near[h, :, DV:VW] = dot(score_b, g_b, TN)
        gs_a = jnp.where(same, dot(g_a, v_a, NT), 0.0)
        gs_b = jnp.where(same, dot(g_b, v_b, NT), 0.0)
        dq_near[h] = dot(split(jnp.concatenate([gs_a, gs_b], axis=1)), k_2, NN)
        dk_near[h] = factor * shrink * dot(split(jnp.concatenate([gs_a, gs_b], axis=0)), q_2, TN)

    def finish(h):
        far_arrival(h).wait_recv()
        q_f = rx[h, :, 0:KW].astype(F32)
        k_f = rx[h, :, KW : 2 * KW].astype(F32)
        v = rx[h, :, 3 * KW : W]
        g = g_ref[0, :, lanes(h, VW)]
        growth = grow[h]
        to_end = end[h]
        q_t = q_f * growth
        k_e = k_f * to_end * tail_w
        f_in = into[0, h]
        b_in = into[1, h]
        f_end = loc[0, h] + pass_state * decay[h] * f_in
        state = both(spread, split(f_in))
        carry = both(spread, split(b_in))
        far = dot(split(q_t * head_w), state, NN)
        out_ref[0, :, lanes(h, VW)] = (factor * (near[h] + far)).astype(BF16)
        dq = factor * growth * (dq_near[h] + dot(g, state, NT) * head_w)
        dk = dk_near[h] + to_end * dot(v, carry, NT) * tail_w
        dv = factor * dv_near[h] + dot(split(k_e), carry, NN)
        log_grad = q_f * dq - k_f * dk
        sums = dot(jnp.ones((8, DV), BF16), split(f_end * b_in), NT)
        dd = dot(later, split(log_grad), NN) + sums[0:1] * tail_w
        sy[h, :, 0:KW] = dq.astype(BF16)
        sy[h, :, KW : 2 * KW] = dk.astype(BF16)
        sy[h, :, 2 * KW : 3 * KW] = dd.astype(BF16)
        sy[h, :, 3 * KW : W] = dv.astype(BF16)
        ry[h, my_rows(me), :] = sy[h, my_rows(me), :]
        for r in range(1, n_dp):
            exchange(sy, ry, y_send, y_recv, h, r).start()

    def relay(h):
        mate(h).wait_recv()

        @pl.when(has_from)
        def _():
            chain(h).wait_recv()

        here = mate_in[h, 0] + mate_in[h, 1] * chain_in[h]
        into[own, h] = here

        @pl.when(has_to)
        def _():
            chain_out[h] = loc[own, h] + pass_own * decay[h] * here
            chain(h).start()

        far(h).start()

    lag = jnp.maximum(hops, chips - 1 - hops) + 1

    def step(t, carry):
        passed = t - hops
        ready = t - lag

        @pl.when(t < pairs)
        def _():
            nearby(t)

        @pl.when((passed >= 0) & (passed < pairs))
        def _():
            relay(passed)

        @pl.when((ready >= 0) & (ready < pairs))
        def _():
            finish(ready)

        return carry

    lax.fori_loop(0, chips + pairs, step, 0)

    def wait_back(h, carry):
        for r in range(1, n_dp):
            arrival(sy, ry, y_send, y_recv, h, r).wait_recv()
        return carry

    lax.fori_loop(0, pairs, wait_back, 0)

    def drain(h, carry):
        for r in range(1, n_dp):
            exchange(sx, rx, x_send, x_recv, h, r).wait_send()
            exchange(sy, ry, y_send, y_recv, h, r).wait_send()

        mate(h).wait_send()
        far(h).wait_send()

        @pl.when(has_to)
        def _():
            chain(h).wait_send()

        return carry

    lax.fori_loop(0, pairs, drain, 0)

    @pl.when(has_next)
    def _():
        doc_up().wait_send()

    @pl.when(has_prev)
    def _():
        doc_down().wait_send()


def unpack(pairs, order_ref, ry, rows_ref, out_ref, dq_ref, dk_ref, dv_ref, dd_ref,
           buf, rows_v, dq_v, dk_v, dv_v, dd_v, in_sem, out_sem, rows_sem):
    me = lax.axis_index("dp")
    blocks = rows_ref.shape[1] // BLK
    rows_in = pltpu.make_async_copy(rows_ref, rows_v, rows_sem.at[0])
    rows_in.start()
    rows_out = pltpu.make_async_copy(rows_v, out_ref, rows_sem.at[1])
    fetches = []
    for j in range(blocks):
        here = pl.ds(pl.multiple_of(order_ref[me, 0, j] * BLK, BLK), BLK)
        fetches.append(pltpu.make_async_copy(ry.at[:, here, :], buf.at[j], in_sem.at[j]))
        fetches[j].start()
    rows_in.wait()
    rows_out.start()
    stores = []
    for j in range(blocks):
        fetches[j].wait()
        there = slice(j * BLK, (j + 1) * BLK)
        for h in range(pairs):
            key, value = slice(h * KW, (h + 1) * KW), slice(h * VW, (h + 1) * VW)
            dq_v[0, there, key] = buf[j, h, :, 0:KW]
            dk_v[0, there, key] = buf[j, h, :, KW : 2 * KW]
            dd_v[0, there, key] = buf[j, h, :, 2 * KW : 3 * KW]
            dv_v[0, there, value] = buf[j, h, :, 3 * KW : W]
        for i, (src, dst) in enumerate(((dq_v, dq_ref), (dk_v, dk_ref), (dv_v, dv_ref), (dd_v, dd_ref))):
            store = pltpu.make_async_copy(src.at[:, there, :], dst.at[:, there, :], out_sem.at[j, i])
            store.start()
            stores.append(store)
    for store in stores:
        store.wait()
    rows_out.wait()


def body(n_dp, n_ctx, query_rows, key_rows, value_rows, log_decay, out_grad, doc_ids, block_order):
    rows, hk = query_rows.shape[1:]
    hv = value_rows.shape[2]
    pairs = hk // KW
    vmem = pl.BlockSpec(memory_space=pltpu.VMEM)
    keys = jax.ShapeDtypeStruct((1, rows, hk), BF16)
    values = jax.ShapeDtypeStruct((1, rows, hv), BF16)
    dma = pltpu.SemaphoreType.DMA
    rows_out, back = pl.pallas_call(
        functools.partial(kernel, n_dp, n_ctx),
        out_shape=(values, jax.ShapeDtypeStruct((pairs, rows, W), BF16)),
        in_specs=[pl.BlockSpec(memory_space=pltpu.HBM)] * 7,
        out_specs=(vmem,) * 2,
        scratch_shapes=[
            pltpu.SMEM(block_order.shape, jnp.int32),
            pltpu.VMEM((1, rows), jnp.int32),
            pltpu.VMEM((1, rows, hk), BF16),
            pltpu.VMEM((1, rows, hk), BF16),
            pltpu.VMEM((1, rows, hv), BF16),
            pltpu.VMEM((1, rows, hk), BF16),
            pltpu.VMEM((1, rows, hv), BF16),
            dma((7,)),
            pltpu.VMEM((pairs, KW, DV), F32),
            pltpu.VMEM((pairs, rows, KW), F32),
            pltpu.VMEM((pairs, rows, KW), F32),
            pltpu.VMEM((pairs, rows, VW), F32),
            pltpu.VMEM((pairs, rows, VW), F32),
            pltpu.VMEM((pairs, rows, KW), F32),
            pltpu.VMEM((pairs, rows, KW), F32),
            pltpu.VMEM((pairs, rows, W), BF16),
            pltpu.VMEM((pairs, rows, W), BF16),
            pltpu.VMEM((pairs, rows, W), BF16),
            pltpu.VMEM((2, pairs, KW, DV), F32),
            pltpu.VMEM((2, pairs, KW, DV), F32),
            pltpu.VMEM((pairs, 2, KW, DV), F32),
            pltpu.VMEM((pairs, 2, KW, DV), F32),
            pltpu.VMEM((pairs, KW, DV), F32),
            pltpu.VMEM((pairs, KW, DV), F32),
            pltpu.VMEM((1, rows), jnp.int32),
            pltpu.VMEM((1, rows), jnp.int32),
            dma((pairs, n_dp)), dma((pairs, n_dp)), dma((pairs, n_dp)), dma((pairs, n_dp)),
            dma((pairs,)), dma((pairs,)), dma((pairs,)), dma((pairs,)), dma((pairs,)), dma((pairs,)),
            dma((2,)), dma((2,)),
        ],
        compiler_params=pltpu.CompilerParams(
            collective_id=0, has_side_effects=True, vmem_limit_bytes=56 * 1024 * 1024
        ),
    )(block_order, doc_ids, query_rows, key_rows, value_rows, log_decay, out_grad)
    hbm = pl.BlockSpec(memory_space=pltpu.HBM)
    key_rows_v, value_rows_v = pltpu.VMEM((1, rows, hk), BF16), pltpu.VMEM((1, rows, hv), BF16)
    return pl.pallas_call(
        functools.partial(unpack, pairs),
        out_shape=(values, keys, keys, values, keys),
        in_specs=[pl.BlockSpec(memory_space=pltpu.SMEM), hbm, hbm],
        out_specs=(hbm,) * 5,
        scratch_shapes=[
            pltpu.VMEM((rows // BLK, pairs, BLK, W), BF16),
            value_rows_v, key_rows_v, key_rows_v, value_rows_v, key_rows_v,
            dma((rows // BLK,)), dma((rows // BLK, 4)), dma((2,)),
        ],
        compiler_params=pltpu.CompilerParams(vmem_limit_bytes=56 * 1024 * 1024),
    )(block_order, back, rows_out)


def solution(mesh):
    placed = P("dp", "ctx", None)
    return jax.shard_map(
        functools.partial(body, mesh.shape["dp"], mesh.shape["ctx"]),
        mesh=mesh,
        in_specs=(placed,) * 5 + (P("dp", "ctx"), P(None, "ctx", None)),
        out_specs=(placed,) * 5,
        check_vma=False,
    )
```

```python
import functools

import jax
import jax.numpy as jnp
from jax import lax
from jax.experimental import pallas as pl
from jax.experimental.pallas import tpu as pltpu
from jax.sharding import PartitionSpec as P

DK = 64
DV = 128
BLK = 32
KW = 2 * DK
VW = 2 * DV
W = 3 * KW + VW
TILE = 8
FLIGHT = 3
MESH = pl.DeviceIdType.MESH
F32 = jnp.float32
BF16 = jnp.bfloat16

NN = (((1,), (0,)), ((), ()))
NT = (((1,), (1,)), ((), ()))
TN = (((0,), (0,)), ((), ()))


def split(x):
    hi = x.astype(BF16)
    return hi, (x - hi.astype(F32)).astype(BF16)


def dot(a, b, dims):
    a = a if isinstance(a, tuple) else (a,)
    b = b if isinstance(b, tuple) else (b,)
    total = None
    for i, left in enumerate(a):
        for j, right in enumerate(b):
            if i + j > 1:
                continue
            term = lax.dot_general(left, right, dims, preferred_element_type=F32)
            total = term if total is None else total + term
    return total


def both(fn, pair):
    return tuple(fn(x) for x in pair)


def kernel(
    n_dp, n_ctx, order_hbm, doc_hbm, q_hbm, k_hbm, v_hbm, d_hbm, g_hbm,
    out_ref, dq_ref, dk_ref, dv_ref, dd_ref,
    order_ref, doc_ref, q_ref, k_ref, v_ref, d_ref, g_ref, in_sem, decay, grow, end, near, dv_near, dq_near, dk_near,
    sx, rx, sy, ry, loc, into, mate_out, mate_in, chain_out, chain_in, hop_out, hop_in, before, doc_prev, doc_next,
    x_send, x_recv, y_send, y_recv, mate_send, mate_recv, chain_send, chain_recv, hop_send, hop_recv, far_send, far_recv,
    doc_send, doc_recv,
):
    me = lax.axis_index("dp")
    pos = lax.axis_index("ctx")
    rows = q_hbm.shape[1]
    pairs = q_hbm.shape[2] // KW
    blocks = rows // BLK
    per = blocks // n_dp
    part = per * BLK
    chips = n_ctx // 2
    has_prev = pos > 0
    has_next = pos < n_ctx - 1
    core = lax.rem(pos, 2)
    own = 1 - core
    mate_pos = pos + 1 - 2 * core
    ahead = 4 * core - 2
    chip = pos // 2
    behind = jnp.where(core == 1, chip, chips - 1 - chip)
    spans = spans_of(n_ctx)

    def has_from(span):
        return behind >= span

    def has_to(span):
        return behind + span < chips

    barrier = pltpu.get_barrier_semaphore()
    for r in range(1, n_dp):
        peer = lax.rem(me + r, n_dp)
        pl.semaphore_signal(barrier, inc=1, device_id={"dp": peer}, device_id_type=MESH)

    peers = n_dp - 1
    for step in (-1, 1, *(sign * 2 * span for span in sorted({1, 2, *spans}) for sign in (-1, 1))):
        there = (pos + step >= 0) & (pos + step < n_ctx)
        peers = peers + there.astype(jnp.int32)

        @pl.when(there)
        def _():
            pl.semaphore_signal(barrier, inc=1, device_id={"ctx": pos + step}, device_id_type=MESH)

    fetches = [
        pltpu.make_async_copy(src, dst, in_sem.at[i])
        for i, (src, dst) in enumerate((
            (order_hbm, order_ref), (q_hbm, q_ref), (k_hbm, k_ref), (d_hbm, d_ref),
            (v_hbm, v_ref), (doc_hbm, doc_ref), (g_hbm, g_ref),
        ))
    ]
    for fetch in fetches:
        fetch.start()

    def my_rows(index):
        return pl.ds(pl.multiple_of(index * part, part), part)

    def lanes(h, width):
        return pl.ds(pl.multiple_of(h * width, width), width)

    for fetch in fetches[:5]:
        fetch.wait()

    @pl.when(jnp.logical_not(has_prev))
    def _():
        doc_prev[...] = jnp.full_like(doc_prev, -1)

    @pl.when(jnp.logical_not(has_next))
    def _():
        doc_next[...] = jnp.full_like(doc_next, -1)

    for span in (1, 2):
        @pl.when(jnp.logical_not(has_from(span)))
        def _():
            chain_in[span - 1] = jnp.zeros_like(chain_in[span - 1])

    for i, span in enumerate(spans):
        @pl.when(jnp.logical_not(has_from(span)))
        def _():
            hop_in[i] = jnp.zeros_like(hop_in[i])

    order = [order_ref[me, 0, j] for j in range(blocks)]

    def piece(j):
        return slice(j * BLK, (j + 1) * BLK)

    def stage(h, carry):
        for src, width, at in ((q_ref, KW, 0), (k_ref, KW, KW), (d_ref, KW, 2 * KW), (v_ref, VW, 3 * KW)):
            parts = [src[0, piece(j), lanes(h, width)] for j in range(blocks)]
            for dest in range(blocks):
                chosen = parts[0]
                for j in range(1, blocks):
                    chosen = lax.select(order[j] == dest, parts[j], chosen)
                sx[h, piece(dest), at : at + width] = chosen
        return carry

    lax.fori_loop(0, pairs, stage, 0)

    pl.semaphore_wait(barrier, peers)

    def exchange(src, dst, send, recv, h, r):
        peer = lax.rem(me + r, n_dp)
        return pltpu.make_async_remote_copy(
            src_ref=src.at[h, my_rows(peer), :],
            dst_ref=dst.at[h, my_rows(me), :],
            send_sem=send.at[h, r],
            recv_sem=recv.at[h, r],
            device_id={"dp": peer},
            device_id_type=MESH,
        )

    def arrival(src, dst, send, recv, h, r):
        source = lax.rem(me + n_dp - r, n_dp)
        return pltpu.make_async_remote_copy(
            src_ref=src.at[h, my_rows(source), :],
            dst_ref=dst.at[h, my_rows(source), :],
            send_sem=send.at[h, r],
            recv_sem=recv.at[h, r],
            device_id={"dp": source},
            device_id_type=MESH,
        )

    def to_ctx(src, dst, send, recv, there):
        return pltpu.make_async_remote_copy(
            src_ref=src, dst_ref=dst, send_sem=send, recv_sem=recv,
            device_id={"ctx": there}, device_id_type=MESH,
        )

    def doc_up():
        return to_ctx(doc_ref, doc_prev, doc_send.at[0], doc_recv.at[0], pos + 1)

    def doc_down():
        return to_ctx(doc_ref, doc_next, doc_send.at[1], doc_recv.at[1], pos - 1)

    def mate(h):
        return to_ctx(mate_out.at[h], mate_in.at[h], mate_send.at[h], mate_recv.at[h], mate_pos)

    def chain(h, span):
        size = KW + TILE if span == 1 or spans else KW
        return to_ctx(
            chain_out.at[h, 0:size], chain_in.at[span - 1, h, 0:size],
            chain_send.at[h, span - 1], chain_recv.at[h, span - 1], pos + ahead * span,
        )

    def hop(h, i):
        return to_ctx(hop_out.at[i, h], hop_in.at[i, h], hop_send.at[h, i], hop_recv.at[h, i], pos + ahead * spans[i])

    def far(h):
        return to_ctx(before.at[h], into.at[own, h], far_send.at[h], far_recv.at[h], mate_pos)

    def far_arrival(h):
        return to_ctx(before.at[h], into.at[1 - own, h], far_send.at[h], far_recv.at[h], mate_pos)

    def launch(h, carry):
        for r in range(1, n_dp):
            exchange(sx, rx, x_send, x_recv, h, r).start()
        rx[h, my_rows(me), :] = sx[h, my_rows(me), :]
        return carry

    lax.fori_loop(0, pairs, launch, 0)

    for fetch in fetches[5:]:
        fetch.wait()

    @pl.when(has_next)
    def _():
        doc_up().start()

    @pl.when(has_prev)
    def _():
        doc_down().start()

    @pl.when(has_prev)
    def _():
        doc_up().wait_recv()

    @pl.when(has_next)
    def _():
        doc_down().wait_recv()

    doc_row = jnp.broadcast_to(doc_ref[...].astype(F32), (rows, rows))
    doc_col = doc_row.T
    first_row = doc_col[0:1, :]
    last_row = doc_col[rows - 1 : rows, :]
    prev_last = jnp.broadcast_to(doc_prev[:, rows - 1 : rows].astype(F32), (1, rows))
    next_first = jnp.broadcast_to(doc_next[:, 0:1].astype(F32), (1, rows))
    use_state = (prev_last == first_row).astype(F32)
    use_carry = (next_first == last_row).astype(F32)
    single = (first_row == last_row).astype(F32)
    pass_state = single * use_state
    pass_carry = single * use_carry
    pass_own = jnp.where(core == 1, pass_state, pass_carry)
    pass_mate = jnp.where(core == 1, pass_carry, pass_state)
    in_first = (doc_col == first_row).astype(F32)
    in_last = (doc_col == last_row).astype(F32)
    head_w = in_first * use_state
    tail_w = in_last * use_carry
    row_id = lax.broadcasted_iota(jnp.int32, (rows, rows), 0)
    lane_id = lax.broadcasted_iota(jnp.int32, (rows, rows), 1)
    same = (doc_row == doc_col) & (row_id >= lane_id)
    later = ((doc_row == doc_col) & (row_id <= lane_id)).astype(BF16)
    lower = (row_id >= lane_id).astype(BF16)
    in_a = lax.broadcasted_iota(jnp.int32, (rows, KW), 1) < DK
    factor = DK ** (-0.5)

    def load(h):
        q = rx[h, :, 0:KW]
        k = rx[h, :, KW : 2 * KW]
        d = rx[h, :, 2 * KW : 3 * KW]
        v = rx[h, :, 3 * KW : W]
        g = g_ref[0, :, lanes(h, VW)]
        cum = dot(lower, d, NN)
        total = cum[rows - 1 : rows, :]
        growth = jnp.exp(cum)
        shrink = jnp.exp(-cum)
        to_end = jnp.exp(total - cum)
        grow[h] = growth
        end[h] = to_end
        return q.astype(F32), k.astype(F32), v, g, d, growth, shrink, to_end, jnp.exp(total)

    def fold(wide):
        return jnp.concatenate([wide[0:DK, 0:DV], wide[DK:KW, DV:VW]], axis=0)

    def spread(tall):
        nil = jnp.zeros((DK, DV), tall.dtype)
        top = jnp.concatenate([tall[0:DK], nil], axis=1)
        low = jnp.concatenate([nil, tall[DK:KW]], axis=1)
        return jnp.concatenate([top, low], axis=0)

    def nearby(h):
        for r in range(1, n_dp):
            arrival(sx, rx, x_send, x_recv, h, r).wait_recv()
        q_f, k_f, v, g, d, growth, shrink, to_end, fade = load(h)
        loc[0, h] = fold(dot(split(k_f * to_end * in_last), v, TN))
        loc[1, h] = factor * fold(dot(split(q_f * growth * in_first), g, TN))
        decay[h] = jnp.exp(dot(d, jnp.ones((rows, DV), BF16), TN))
        mate_out[h, 0:KW] = loc[1 - own, h]
        mate_out[h, KW : 2 * KW] = pass_mate * decay[h]
        mate_out[h, 2 * KW : 2 * KW + TILE] = jnp.broadcast_to(pass_mate * fade, (TILE, KW))
        chain_out[h, KW : KW + TILE] = jnp.broadcast_to(pass_own * fade, (TILE, KW))
        mate(h).start()
        q_t = q_f * growth
        k_t = k_f * shrink
        zero = jnp.zeros_like(q_t)
        q_2 = split(jnp.concatenate([jnp.where(in_a, q_t, zero), jnp.where(in_a, zero, q_t)], axis=0))
        k_s = split(k_t)
        k_2 = split(jnp.concatenate([jnp.where(in_a, k_t, zero), jnp.where(in_a, zero, k_t)], axis=0))
        same_2 = jnp.concatenate([same, same], axis=0)
        score_2 = split(jnp.where(same_2, dot(q_2, k_s, NT), 0.0))
        v_a, v_b = v[:, 0:DV], v[:, DV:VW]
        g_a, g_b = g[:, 0:DV], g[:, DV:VW]
        score_a = both(lambda x: x[0:rows], score_2)
        score_b = both(lambda x: x[rows : 2 * rows], score_2)
        near[h, :, 0:DV] = dot(score_a, v_a, NN)
        near[h, :, DV:VW] = dot(score_b, v_b, NN)
        dv_near[h, :, 0:DV] = dot(score_a, g_a, TN)
        dv_near[h, :, DV:VW] = dot(score_b, g_b, TN)
        gs_a = jnp.where(same, dot(g_a, v_a, NT), 0.0)
        gs_b = jnp.where(same, dot(g_b, v_b, NT), 0.0)
        dq_near[h] = dot(split(jnp.concatenate([gs_a, gs_b], axis=1)), k_2, NN)
        dk_near[h] = factor * shrink * dot(split(jnp.concatenate([gs_a, gs_b], axis=0)), q_2, TN)

    def finish(h):
        far_arrival(h).wait_recv()
        q_f = rx[h, :, 0:KW].astype(F32)
        k_f = rx[h, :, KW : 2 * KW].astype(F32)
        v = rx[h, :, 3 * KW : W]
        g = g_ref[0, :, lanes(h, VW)]
        growth = grow[h]
        to_end = end[h]
        q_t = q_f * growth
        k_e = k_f * to_end * tail_w
        f_in = into[0, h]
        b_in = into[1, h]
        f_end = loc[0, h] + pass_state * decay[h] * f_in
        state = both(spread, split(f_in))
        carry = both(spread, split(b_in))
        far = dot(split(q_t * head_w), state, NN)
        out_ref[0, :, lanes(h, VW)] = (factor * (near[h] + far)).astype(BF16)
        dq = factor * growth * (dq_near[h] + dot(g, state, NT) * head_w)
        dk = dk_near[h] + to_end * dot(v, carry, NT) * tail_w
        dv = factor * dv_near[h] + dot(split(k_e), carry, NN)
        log_grad = q_f * dq - k_f * dk
        sums = dot(jnp.ones((8, DV), BF16), split(f_end * b_in), NT)
        dd = dot(later, split(log_grad), NN) + sums[0:1] * tail_w
        sy[h, :, 0:KW] = dq.astype(BF16)
        sy[h, :, KW : 2 * KW] = dk.astype(BF16)
        sy[h, :, 2 * KW : 3 * KW] = dd.astype(BF16)
        sy[h, :, 3 * KW : W] = dv.astype(BF16)
        ry[h, my_rows(me), :] = sy[h, my_rows(me), :]
        for r in range(1, n_dp):
            exchange(sy, ry, y_send, y_recv, h, r).start()

    def column(tile):
        return jnp.broadcast_to(tile[0:1], (DV, KW)).T

    def depart(h):
        mate(h).wait_recv()
        chain_out[h, 0:KW] = loc[own, h] + pass_own * decay[h] * mate_in[h, 0:KW]
        chain_out[h, KW : KW + TILE] = chain_out[h, KW : KW + TILE] * mate_in[h, 2 * KW : 2 * KW + TILE]
        for span in (1, 2):
            @pl.when(has_to(span))
            def _():
                chain(h, span).start()

    def join(h, near_ref, far_ref, i):
        fade = near_ref[KW : KW + TILE]
        state = near_ref[0:KW] + column(fade) * far_ref[0:KW]
        if i < len(spans):
            hop_out[i, h, 0:KW] = state
            hop_out[i, h, KW : KW + TILE] = fade * far_ref[KW : KW + TILE]

            @pl.when(has_to(spans[i]))
            def _():
                hop(h, i).start()
        else:
            before[h] = state
            far(h).start()
            into[own, h] = mate_in[h, 0:KW] + mate_in[h, KW : 2 * KW] * state

    def arrive(h):
        for span in (1, 2):
            @pl.when(has_from(span))
            def _():
                chain(h, span).wait_recv()
        join(h, chain_in.at[0, h], chain_in.at[1, h], 0)

    def widen(h, i):
        @pl.when(has_from(spans[i]))
        def _():
            hop(h, i).wait_recv()
        join(h, hop_out.at[i, h], hop_in.at[i, h], i + 1)

    stages = [(0, nearby), (0, depart), (FLIGHT, arrive)]
    for i in range(len(spans)):
        stages.append(((i + 2) * FLIGHT, functools.partial(widen, i=i)))
    last = stages[-1][0] + 1
    stages.append((last, finish))

    def step(t, carry):
        for lag, stage_of in stages:
            @pl.when((t >= lag) & (t < lag + pairs))
            def _():
                stage_of(t - lag)

        return carry

    lax.fori_loop(0, last + pairs, step, 0)

    @pl.when(has_next)
    def _():
        doc_up().wait_send()

    @pl.when(has_prev)
    def _():
        doc_down().wait_send()

    def home(h, carry):
        mate(h).wait_send()
        far(h).wait_send()
        for span in (1, 2):
            @pl.when(has_to(span))
            def _():
                chain(h, span).wait_send()
        for i, span in enumerate(spans):
            @pl.when(has_to(span))
            def _():
                hop(h, i).wait_send()
        for r in range(1, n_dp):
            exchange(sx, rx, x_send, x_recv, h, r).wait_send()
            exchange(sy, ry, y_send, y_recv, h, r).wait_send()
        for r in range(1, n_dp):
            arrival(sy, ry, y_send, y_recv, h, r).wait_recv()
        for dst, width, at in ((dq_ref, KW, 0), (dk_ref, KW, KW), (dd_ref, KW, 2 * KW), (dv_ref, VW, 3 * KW)):
            parts = [ry[h, piece(j), at : at + width] for j in range(blocks)]
            for j in range(blocks):
                chosen = parts[0]
                for source in range(1, blocks):
                    chosen = lax.select(order[j] == source, parts[source], chosen)
                dst[0, piece(j), lanes(h, width)] = chosen
        return carry

    lax.fori_loop(0, pairs, home, 0)


def store(*refs):
    half = len(refs) // 2
    sem = refs[-1]
    copies = [pltpu.make_async_copy(refs[i], refs[half + i], sem.at[i]) for i in range(half)]
    for copy in copies:
        copy.start()
    for copy in copies:
        copy.wait()


def spans_of(n_ctx):
    chips = n_ctx // 2
    span, spans = 2, []
    while span < chips // 2:
        spans.append(span)
        span *= 2
    return spans


def body(n_dp, n_ctx, query_rows, key_rows, value_rows, log_decay, out_grad, doc_ids, block_order):
    rows, hk = query_rows.shape[1:]
    hv = value_rows.shape[2]
    pairs = hk // KW
    rounds = max(len(spans_of(n_ctx)), 1)
    vmem = pl.BlockSpec(memory_space=pltpu.VMEM)
    keys = jax.ShapeDtypeStruct((1, rows, hk), BF16)
    values = jax.ShapeDtypeStruct((1, rows, hv), BF16)
    outs = (values, keys, keys, values, keys)
    dma = pltpu.SemaphoreType.DMA
    held = pl.pallas_call(
        functools.partial(kernel, n_dp, n_ctx),
        out_shape=tuple(pltpu.VMEM(x.shape, BF16) for x in outs),
        in_specs=[pl.BlockSpec(memory_space=pltpu.HBM)] * 7,
        out_specs=(vmem,) * 5,
        scratch_shapes=[
            pltpu.SMEM(block_order.shape, jnp.int32),
            pltpu.VMEM((1, rows), jnp.int32),
            pltpu.VMEM((1, rows, hk), BF16),
            pltpu.VMEM((1, rows, hk), BF16),
            pltpu.VMEM((1, rows, hv), BF16),
            pltpu.VMEM((1, rows, hk), BF16),
            pltpu.VMEM((1, rows, hv), BF16),
            dma((7,)),
            pltpu.VMEM((pairs, KW, DV), F32),
            pltpu.VMEM((pairs, rows, KW), F32),
            pltpu.VMEM((pairs, rows, KW), F32),
            pltpu.VMEM((pairs, rows, VW), F32),
            pltpu.VMEM((pairs, rows, VW), F32),
            pltpu.VMEM((pairs, rows, KW), F32),
            pltpu.VMEM((pairs, rows, KW), F32),
            pltpu.VMEM((pairs, rows, W), BF16),
            pltpu.VMEM((pairs, rows, W), BF16),
            pltpu.VMEM((pairs, rows, W), BF16),
            pltpu.VMEM((pairs, rows, W), BF16),
            pltpu.VMEM((2, pairs, KW, DV), F32),
            pltpu.VMEM((2, pairs, KW, DV), F32),
            pltpu.VMEM((pairs, 2 * KW + TILE, DV), F32),
            pltpu.VMEM((pairs, 2 * KW + TILE, DV), F32),
            pltpu.VMEM((pairs, KW + TILE, DV), F32),
            pltpu.VMEM((2, pairs, KW + TILE, DV), F32),
            pltpu.VMEM((rounds, pairs, KW + TILE, DV), F32),
            pltpu.VMEM((rounds, pairs, KW + TILE, DV), F32),
            pltpu.VMEM((pairs, KW, DV), F32),
            pltpu.VMEM((1, rows), jnp.int32),
            pltpu.VMEM((1, rows), jnp.int32),
            dma((pairs, n_dp)), dma((pairs, n_dp)), dma((pairs, n_dp)), dma((pairs, n_dp)),
            dma((pairs,)), dma((pairs,)), dma((pairs, 2)), dma((pairs, 2)), dma((pairs, rounds)), dma((pairs, rounds)),
            dma((pairs,)), dma((pairs,)),
            dma((2,)), dma((2,)),
        ],
        compiler_params=pltpu.CompilerParams(
            collective_id=0, has_side_effects=True, vmem_limit_bytes=56 * 1024 * 1024
        ),
    )(block_order, doc_ids, query_rows, key_rows, value_rows, log_decay, out_grad)
    return pl.pallas_call(
        store,
        out_shape=outs,
        in_specs=(vmem,) * 5,
        out_specs=(pl.BlockSpec(memory_space=pltpu.HBM),) * 5,
        scratch_shapes=[dma((5,))],
    )(*(pltpu.with_memory_space_constraint(x, pltpu.VMEM) for x in held))


def solution(mesh):
    placed = P("dp", "ctx", None)
    return jax.shard_map(
        functools.partial(body, mesh.shape["dp"], mesh.shape["ctx"]),
        mesh=mesh,
        in_specs=(placed,) * 5 + (P("dp", "ctx"), P(None, "ctx", None)),
        out_specs=(placed,) * 5,
        check_vma=False,
    )
```

```python
import functools

import jax
import jax.numpy as jnp
from jax import lax
from jax.experimental import pallas as pl
from jax.experimental.pallas import tpu as pltpu
from jax.sharding import PartitionSpec as P

DK = 64
DV = 128
BLK = 32
KW = 2 * DK
VW = 2 * DV
W = 3 * KW + VW
TILE = 8
FLIGHT = 2
MESH = pl.DeviceIdType.MESH
F32 = jnp.float32
BF16 = jnp.bfloat16

NN = (((1,), (0,)), ((), ()))
NT = (((1,), (1,)), ((), ()))
TN = (((0,), (0,)), ((), ()))


def split(x):
    hi = x.astype(BF16)
    return hi, (x - hi.astype(F32)).astype(BF16)


def dot(a, b, dims):
    a = a if isinstance(a, tuple) else (a,)
    b = b if isinstance(b, tuple) else (b,)
    total = None
    for i, left in enumerate(a):
        for j, right in enumerate(b):
            if i + j > 1:
                continue
            term = lax.dot_general(left, right, dims, preferred_element_type=F32)
            total = term if total is None else total + term
    return total


def both(fn, pair):
    return tuple(fn(x) for x in pair)


def kernel(
    n_dp, n_ctx, order_hbm, doc_hbm, q_hbm, k_hbm, v_hbm, d_hbm, g_hbm,
    out_ref, dq_ref, dk_ref, dv_ref, dd_ref,
    order_ref, doc_ref, q_ref, k_ref, v_ref, d_ref, g_ref, in_sem, decay, grow, end, near, dv_near, dq_near, dk_near,
    sx, rx, sy, ry, loc, into, mate_out, mate_in, chain_out, chain_in, skip_out, skip_in, hop_out, hop_in, before, doc_prev, doc_next,
    x_send, x_recv, y_send, y_recv, mate_send, mate_recv, chain_send, chain_recv, skip_send, skip_recv, hop_send, hop_recv, far_send, far_recv,
    doc_send, doc_recv,
):
    me = lax.axis_index("dp")
    pos = lax.axis_index("ctx")
    rows = q_hbm.shape[1]
    pairs = q_hbm.shape[2] // KW
    blocks = rows // BLK
    per = blocks // n_dp
    part = per * BLK
    chips = n_ctx // 2
    has_prev = pos > 0
    has_next = pos < n_ctx - 1
    core = lax.rem(pos, 2)
    own = 1 - core
    mate_pos = pos + 1 - 2 * core
    ahead = 4 * core - 2
    chip = pos // 2
    behind = jnp.where(core == 1, chip, chips - 1 - chip)
    spans = spans_of(n_ctx)

    def has_from(span):
        return behind >= span

    def has_to(span):
        return behind + span < chips

    barrier = pltpu.get_barrier_semaphore()
    for r in range(1, n_dp):
        peer = lax.rem(me + r, n_dp)
        pl.semaphore_signal(barrier, inc=1, device_id={"dp": peer}, device_id_type=MESH)

    peers = n_dp - 1
    for step in (-1, 1, *(sign * 2 * span for span in sorted({1, 2, *spans}) for sign in (-1, 1))):
        there = (pos + step >= 0) & (pos + step < n_ctx)
        peers = peers + there.astype(jnp.int32)

        @pl.when(there)
        def _():
            pl.semaphore_signal(barrier, inc=1, device_id={"ctx": pos + step}, device_id_type=MESH)

    fetches = [
        pltpu.make_async_copy(src, dst, in_sem.at[i])
        for i, (src, dst) in enumerate((
            (order_hbm, order_ref), (q_hbm, q_ref), (k_hbm, k_ref), (d_hbm, d_ref),
            (v_hbm, v_ref), (doc_hbm, doc_ref), (g_hbm, g_ref),
        ))
    ]
    for fetch in fetches:
        fetch.start()

    def my_rows(index):
        return pl.ds(pl.multiple_of(index * part, part), part)

    def lanes(h, width):
        return pl.ds(pl.multiple_of(h * width, width), width)

    for fetch in fetches[:5]:
        fetch.wait()

    @pl.when(jnp.logical_not(has_prev))
    def _():
        doc_prev[...] = jnp.full_like(doc_prev, -1)

    @pl.when(jnp.logical_not(has_next))
    def _():
        doc_next[...] = jnp.full_like(doc_next, -1)

    @pl.when(jnp.logical_not(has_from(1)))
    def _():
        chain_in[...] = jnp.zeros_like(chain_in)

    @pl.when(jnp.logical_not(has_from(2)))
    def _():
        skip_in[...] = jnp.zeros_like(skip_in)

    for i, span in enumerate(spans):
        @pl.when(jnp.logical_not(has_from(span)))
        def _():
            hop_in[i] = jnp.zeros_like(hop_in[i])

    order = [order_ref[me, 0, j] for j in range(blocks)]

    def piece(j):
        return slice(j * BLK, (j + 1) * BLK)

    def stage(h, carry):
        for src, width, at in ((q_ref, KW, 0), (k_ref, KW, KW), (d_ref, KW, 2 * KW), (v_ref, VW, 3 * KW)):
            parts = [src[0, piece(j), lanes(h, width)] for j in range(blocks)]
            for dest in range(blocks):
                chosen = parts[0]
                for j in range(1, blocks):
                    chosen = lax.select(order[j] == dest, parts[j], chosen)
                sx[h, piece(dest), at : at + width] = chosen
        return carry

    lax.fori_loop(0, pairs, stage, 0)

    pl.semaphore_wait(barrier, peers)

    def exchange(src, dst, send, recv, h, r):
        peer = lax.rem(me + r, n_dp)
        return pltpu.make_async_remote_copy(
            src_ref=src.at[h, my_rows(peer), :],
            dst_ref=dst.at[h, my_rows(me), :],
            send_sem=send.at[h, r],
            recv_sem=recv.at[h, r],
            device_id={"dp": peer},
            device_id_type=MESH,
        )

    def arrival(src, dst, send, recv, h, r):
        source = lax.rem(me + n_dp - r, n_dp)
        return pltpu.make_async_remote_copy(
            src_ref=src.at[h, my_rows(source), :],
            dst_ref=dst.at[h, my_rows(source), :],
            send_sem=send.at[h, r],
            recv_sem=recv.at[h, r],
            device_id={"dp": source},
            device_id_type=MESH,
        )

    def to_ctx(src, dst, send, recv, there):
        return pltpu.make_async_remote_copy(
            src_ref=src, dst_ref=dst, send_sem=send, recv_sem=recv,
            device_id={"ctx": there}, device_id_type=MESH,
        )

    def doc_up():
        return to_ctx(doc_ref, doc_prev, doc_send.at[0], doc_recv.at[0], pos + 1)

    def doc_down():
        return to_ctx(doc_ref, doc_next, doc_send.at[1], doc_recv.at[1], pos - 1)

    def mate(h):
        return to_ctx(mate_out.at[h], mate_in.at[h], mate_send.at[h], mate_recv.at[h], mate_pos)

    def chain(h):
        return to_ctx(chain_out.at[h], chain_in.at[h], chain_send.at[h], chain_recv.at[h], pos + ahead)

    def skip(h):
        return to_ctx(skip_out.at[h], skip_in.at[h], skip_send.at[h], skip_recv.at[h], pos + 2 * ahead)

    def hop(h, i):
        return to_ctx(hop_out.at[i, h], hop_in.at[i, h], hop_send.at[h, i], hop_recv.at[h, i], pos + ahead * spans[i])

    def far(h):
        return to_ctx(before.at[h], into.at[own, h], far_send.at[h], far_recv.at[h], mate_pos)

    def far_arrival(h):
        return to_ctx(before.at[h], into.at[1 - own, h], far_send.at[h], far_recv.at[h], mate_pos)

    def launch(h, carry):
        for r in range(1, n_dp):
            exchange(sx, rx, x_send, x_recv, h, r).start()
        rx[h, my_rows(me), :] = sx[h, my_rows(me), :]
        return carry

    lax.fori_loop(0, pairs, launch, 0)

    for fetch in fetches[5:]:
        fetch.wait()

    @pl.when(has_next)
    def _():
        doc_up().start()

    @pl.when(has_prev)
    def _():
        doc_down().start()

    @pl.when(has_prev)
    def _():
        doc_up().wait_recv()

    @pl.when(has_next)
    def _():
        doc_down().wait_recv()

    doc_row = jnp.broadcast_to(doc_ref[...].astype(F32), (rows, rows))
    doc_col = doc_row.T
    first_row = doc_col[0:1, :]
    last_row = doc_col[rows - 1 : rows, :]
    prev_last = jnp.broadcast_to(doc_prev[:, rows - 1 : rows].astype(F32), (1, rows))
    next_first = jnp.broadcast_to(doc_next[:, 0:1].astype(F32), (1, rows))
    use_state = (prev_last == first_row).astype(F32)
    use_carry = (next_first == last_row).astype(F32)
    single = (first_row == last_row).astype(F32)
    pass_state = single * use_state
    pass_carry = single * use_carry
    pass_own = jnp.where(core == 1, pass_state, pass_carry)
    pass_mate = jnp.where(core == 1, pass_carry, pass_state)
    in_first = (doc_col == first_row).astype(F32)
    in_last = (doc_col == last_row).astype(F32)
    head_w = in_first * use_state
    tail_w = in_last * use_carry
    row_id = lax.broadcasted_iota(jnp.int32, (rows, rows), 0)
    lane_id = lax.broadcasted_iota(jnp.int32, (rows, rows), 1)
    same = (doc_row == doc_col) & (row_id >= lane_id)
    later = ((doc_row == doc_col) & (row_id <= lane_id)).astype(BF16)
    lower = (row_id >= lane_id).astype(BF16)
    in_a = lax.broadcasted_iota(jnp.int32, (rows, KW), 1) < DK
    factor = DK ** (-0.5)

    def load(h):
        q = rx[h, :, 0:KW]
        k = rx[h, :, KW : 2 * KW]
        d = rx[h, :, 2 * KW : 3 * KW]
        v = rx[h, :, 3 * KW : W]
        g = g_ref[0, :, lanes(h, VW)]
        cum = dot(lower, d, NN)
        total = cum[rows - 1 : rows, :]
        growth = jnp.exp(cum)
        shrink = jnp.exp(-cum)
        to_end = jnp.exp(total - cum)
        grow[h] = growth
        end[h] = to_end
        return q.astype(F32), k.astype(F32), v, g, d, growth, shrink, to_end, jnp.exp(total)

    def fold(wide):
        return jnp.concatenate([wide[0:DK, 0:DV], wide[DK:KW, DV:VW]], axis=0)

    def spread(tall):
        nil = jnp.zeros((DK, DV), tall.dtype)
        top = jnp.concatenate([tall[0:DK], nil], axis=1)
        low = jnp.concatenate([nil, tall[DK:KW]], axis=1)
        return jnp.concatenate([top, low], axis=0)

    def nearby(h):
        for r in range(1, n_dp):
            arrival(sx, rx, x_send, x_recv, h, r).wait_recv()
        q_f, k_f, v, g, d, growth, shrink, to_end, fade = load(h)
        loc[0, h] = fold(dot(split(k_f * to_end * in_last), v, TN))
        loc[1, h] = factor * fold(dot(split(q_f * growth * in_first), g, TN))
        decay[h] = jnp.exp(dot(d, jnp.ones((rows, DV), BF16), TN))
        mate_out[h, 0:KW] = loc[1 - own, h]
        mate_out[h, KW : 2 * KW] = pass_mate * decay[h]
        mate_out[h, 2 * KW : 2 * KW + TILE] = jnp.broadcast_to(pass_mate * fade, (TILE, KW))
        chain_out[h, KW : KW + TILE] = jnp.broadcast_to(pass_own * fade, (TILE, KW))
        mate(h).start()
        q_t = q_f * growth
        k_t = k_f * shrink
        zero = jnp.zeros_like(q_t)
        q_2 = split(jnp.concatenate([jnp.where(in_a, q_t, zero), jnp.where(in_a, zero, q_t)], axis=0))
        k_s = split(k_t)
        k_2 = split(jnp.concatenate([jnp.where(in_a, k_t, zero), jnp.where(in_a, zero, k_t)], axis=0))
        same_2 = jnp.concatenate([same, same], axis=0)
        score_2 = split(jnp.where(same_2, dot(q_2, k_s, NT), 0.0))
        v_a, v_b = v[:, 0:DV], v[:, DV:VW]
        g_a, g_b = g[:, 0:DV], g[:, DV:VW]
        score_a = both(lambda x: x[0:rows], score_2)
        score_b = both(lambda x: x[rows : 2 * rows], score_2)
        near[h, :, 0:DV] = dot(score_a, v_a, NN)
        near[h, :, DV:VW] = dot(score_b, v_b, NN)
        dv_near[h, :, 0:DV] = dot(score_a, g_a, TN)
        dv_near[h, :, DV:VW] = dot(score_b, g_b, TN)
        gs_a = jnp.where(same, dot(g_a, v_a, NT), 0.0)
        gs_b = jnp.where(same, dot(g_b, v_b, NT), 0.0)
        dq_near[h] = dot(split(jnp.concatenate([gs_a, gs_b], axis=1)), k_2, NN)
        dk_near[h] = factor * shrink * dot(split(jnp.concatenate([gs_a, gs_b], axis=0)), q_2, TN)

    def finish(h):
        far_arrival(h).wait_recv()
        q_f = rx[h, :, 0:KW].astype(F32)
        k_f = rx[h, :, KW : 2 * KW].astype(F32)
        v = rx[h, :, 3 * KW : W]
        g = g_ref[0, :, lanes(h, VW)]
        growth = grow[h]
        to_end = end[h]
        q_t = q_f * growth
        k_e = k_f * to_end * tail_w
        f_in = into[0, h]
        b_in = into[1, h]
        f_end = loc[0, h] + pass_state * decay[h] * f_in
        state = both(spread, split(f_in))
        carry = both(spread, split(b_in))
        far = dot(split(q_t * head_w), state, NN)
        out_ref[0, :, lanes(h, VW)] = (factor * (near[h] + far)).astype(BF16)
        dq = factor * growth * (dq_near[h] + dot(g, state, NT) * head_w)
        dk = dk_near[h] + to_end * dot(v, carry, NT) * tail_w
        dv = factor * dv_near[h] + dot(split(k_e), carry, NN)
        log_grad = q_f * dq - k_f * dk
        sums = dot(jnp.ones((8, DV), BF16), split(f_end * b_in), NT)
        dd = dot(later, split(log_grad), NN) + sums[0:1] * tail_w
        sy[h, :, 0:KW] = dq.astype(BF16)
        sy[h, :, KW : 2 * KW] = dk.astype(BF16)
        sy[h, :, 2 * KW : 3 * KW] = dd.astype(BF16)
        sy[h, :, 3 * KW : W] = dv.astype(BF16)
        ry[h, my_rows(me), :] = sy[h, my_rows(me), :]
        for r in range(1, n_dp):
            exchange(sy, ry, y_send, y_recv, h, r).start()

    def column(tile):
        return jnp.broadcast_to(tile[0:1], (DV, KW)).T

    def depart(h):
        mate(h).wait_recv()
        chain_out[h, 0:KW] = loc[own, h] + pass_own * decay[h] * mate_in[h, 0:KW]
        chain_out[h, KW : KW + TILE] = chain_out[h, KW : KW + TILE] * mate_in[h, 2 * KW : 2 * KW + TILE]

        @pl.when(has_to(1))
        def _():
            chain(h).start()

        @pl.when(has_to(2))
        def _():
            skip_out[h] = chain_out[h, 0 : skip_out.shape[1]].astype(skip_out.dtype)
            skip(h).start()

    def join(h, near_ref, far_ref, i):
        fade = near_ref[KW : KW + TILE]
        state = near_ref[0:KW] + column(fade) * far_ref[0:KW].astype(F32)
        if i < len(spans):
            hop_out[i, h, 0:KW] = state
            hop_out[i, h, KW : KW + TILE] = fade * far_ref[KW : KW + TILE]

            @pl.when(has_to(spans[i]))
            def _():
                hop(h, i).start()
        else:
            before[h] = state
            far(h).start()
            into[own, h] = mate_in[h, 0:KW] + mate_in[h, KW : 2 * KW] * state

    def arrive(h):
        @pl.when(has_from(1))
        def _():
            chain(h).wait_recv()

        @pl.when(has_from(2))
        def _():
            skip(h).wait_recv()

        join(h, chain_in.at[h], skip_in.at[h], 0)

    def widen(h, i):
        @pl.when(has_from(spans[i]))
        def _():
            hop(h, i).wait_recv()
        join(h, hop_out.at[i, h], hop_in.at[i, h], i + 1)

    stages = [(0, nearby), (0, depart), (FLIGHT, arrive)]
    for i in range(len(spans)):
        stages.append(((i + 2) * FLIGHT, functools.partial(widen, i=i)))
    last = stages[-1][0] + 1
    stages.insert(2, (last, finish))

    def step(t, carry):
        for lag, stage_of in stages:
            @pl.when((t >= lag) & (t < lag + pairs))
            def _():
                stage_of(t - lag)

        return carry

    lax.fori_loop(0, last + pairs, step, 0)

    @pl.when(has_next)
    def _():
        doc_up().wait_send()

    @pl.when(has_prev)
    def _():
        doc_down().wait_send()

    def home(h, carry):
        mate(h).wait_send()
        far(h).wait_send()

        @pl.when(has_to(1))
        def _():
            chain(h).wait_send()

        @pl.when(has_to(2))
        def _():
            skip(h).wait_send()

        for i, span in enumerate(spans):
            @pl.when(has_to(span))
            def _():
                hop(h, i).wait_send()
        for r in range(1, n_dp):
            exchange(sx, rx, x_send, x_recv, h, r).wait_send()
            exchange(sy, ry, y_send, y_recv, h, r).wait_send()
        for r in range(1, n_dp):
            arrival(sy, ry, y_send, y_recv, h, r).wait_recv()
        for dst, width, at in ((dq_ref, KW, 0), (dk_ref, KW, KW), (dd_ref, KW, 2 * KW), (dv_ref, VW, 3 * KW)):
            parts = [ry[h, piece(j), at : at + width] for j in range(blocks)]
            for j in range(blocks):
                chosen = parts[0]
                for source in range(1, blocks):
                    chosen = lax.select(order[j] == source, parts[source], chosen)
                dst[0, piece(j), lanes(h, width)] = chosen
        return carry

    lax.fori_loop(0, pairs, home, 0)


def store(*refs):
    half = len(refs) // 2
    sem = refs[-1]
    copies = [pltpu.make_async_copy(refs[i], refs[half + i], sem.at[i]) for i in range(half)]
    for copy in copies:
        copy.start()
    for copy in copies:
        copy.wait()


def spans_of(n_ctx):
    chips = n_ctx // 2
    span, spans = 2, []
    while span < chips // 2:
        spans.append(span)
        span *= 2
    return spans


def body(n_dp, n_ctx, query_rows, key_rows, value_rows, log_decay, out_grad, doc_ids, block_order):
    rows, hk = query_rows.shape[1:]
    hv = value_rows.shape[2]
    pairs = hk // KW
    rounds = max(len(spans_of(n_ctx)), 1)
    skipped = pltpu.VMEM((pairs, KW + TILE, DV), F32) if spans_of(n_ctx) else pltpu.VMEM((pairs, KW, DV), BF16)
    vmem = pl.BlockSpec(memory_space=pltpu.VMEM)
    keys = jax.ShapeDtypeStruct((1, rows, hk), BF16)
    values = jax.ShapeDtypeStruct((1, rows, hv), BF16)
    outs = (values, keys, keys, values, keys)
    dma = pltpu.SemaphoreType.DMA
    held = pl.pallas_call(
        functools.partial(kernel, n_dp, n_ctx),
        out_shape=tuple(pltpu.VMEM(x.shape, BF16) for x in outs),
        in_specs=[pl.BlockSpec(memory_space=pltpu.HBM)] * 7,
        out_specs=(vmem,) * 5,
        scratch_shapes=[
            pltpu.SMEM(block_order.shape, jnp.int32),
            pltpu.VMEM((1, rows), jnp.int32),
            pltpu.VMEM((1, rows, hk), BF16),
            pltpu.VMEM((1, rows, hk), BF16),
            pltpu.VMEM((1, rows, hv), BF16),
            pltpu.VMEM((1, rows, hk), BF16),
            pltpu.VMEM((1, rows, hv), BF16),
            dma((7,)),
            pltpu.VMEM((pairs, KW, DV), F32),
            pltpu.VMEM((pairs, rows, KW), F32),
            pltpu.VMEM((pairs, rows, KW), F32),
            pltpu.VMEM((pairs, rows, VW), F32),
            pltpu.VMEM((pairs, rows, VW), F32),
            pltpu.VMEM((pairs, rows, KW), F32),
            pltpu.VMEM((pairs, rows, KW), F32),
            pltpu.VMEM((pairs, rows, W), BF16),
            pltpu.VMEM((pairs, rows, W), BF16),
            pltpu.VMEM((pairs, rows, W), BF16),
            pltpu.VMEM((pairs, rows, W), BF16),
            pltpu.VMEM((2, pairs, KW, DV), F32),
            pltpu.VMEM((2, pairs, KW, DV), F32),
            pltpu.VMEM((pairs, 2 * KW + TILE, DV), F32),
            pltpu.VMEM((pairs, 2 * KW + TILE, DV), F32),
            pltpu.VMEM((pairs, KW + TILE, DV), F32),
            pltpu.VMEM((pairs, KW + TILE, DV), F32),
            skipped, skipped,
            pltpu.VMEM((rounds, pairs, KW + TILE, DV), F32),
            pltpu.VMEM((rounds, pairs, KW + TILE, DV), F32),
            pltpu.VMEM((pairs, KW, DV), F32),
            pltpu.VMEM((1, rows), jnp.int32),
            pltpu.VMEM((1, rows), jnp.int32),
            dma((pairs, n_dp)), dma((pairs, n_dp)), dma((pairs, n_dp)), dma((pairs, n_dp)),
            dma((pairs,)), dma((pairs,)), dma((pairs,)), dma((pairs,)), dma((pairs,)), dma((pairs,)), dma((pairs, rounds)), dma((pairs, rounds)),
            dma((pairs,)), dma((pairs,)),
            dma((2,)), dma((2,)),
        ],
        compiler_params=pltpu.CompilerParams(
            collective_id=0, has_side_effects=True, vmem_limit_bytes=56 * 1024 * 1024
        ),
    )(block_order, doc_ids, query_rows, key_rows, value_rows, log_decay, out_grad)
    return pl.pallas_call(
        store,
        out_shape=outs,
        in_specs=(vmem,) * 5,
        out_specs=(pl.BlockSpec(memory_space=pltpu.HBM),) * 5,
        scratch_shapes=[dma((5,))],
    )(*(pltpu.with_memory_space_constraint(x, pltpu.VMEM) for x in held))


def solution(mesh):
    placed = P("dp", "ctx", None)
    return jax.shard_map(
        functools.partial(body, mesh.shape["dp"], mesh.shape["ctx"]),
        mesh=mesh,
        in_specs=(placed,) * 5 + (P("dp", "ctx"), P(None, "ctx", None)),
        out_specs=(placed,) * 5,
        check_vma=False,
    )
```

```python
import functools

import jax
import jax.numpy as jnp
from jax import lax
from jax.experimental import pallas as pl
from jax.experimental.pallas import tpu as pltpu
from jax.sharding import PartitionSpec as P

DK = 64
DV = 128
BLK = 32
KW = 2 * DK
VW = 2 * DV
W = 3 * KW + VW
TILE = 8
FLIGHT = 2
MESH = pl.DeviceIdType.MESH
F32 = jnp.float32
BF16 = jnp.bfloat16

NN = (((1,), (0,)), ((), ()))
NT = (((1,), (1,)), ((), ()))
TN = (((0,), (0,)), ((), ()))


def split(x):
    hi = x.astype(BF16)
    return hi, (x - hi.astype(F32)).astype(BF16)


def dot(a, b, dims):
    a = a if isinstance(a, tuple) else (a,)
    b = b if isinstance(b, tuple) else (b,)
    total = None
    for i, left in enumerate(a):
        for j, right in enumerate(b):
            if i + j > 1:
                continue
            term = lax.dot_general(left, right, dims, preferred_element_type=F32)
            total = term if total is None else total + term
    return total


def both(fn, pair):
    return tuple(fn(x) for x in pair)


def kernel(
    n_dp, n_ctx, order_hbm, doc_hbm, q_hbm, k_hbm, v_hbm, d_hbm, g_hbm,
    out_ref, dq_ref, dk_ref, dv_ref, dd_ref,
    order_ref, doc_ref, q_ref, k_ref, v_ref, d_ref, g_ref, in_sem, decay, grow, end, near, dv_near, dq_near, dk_near,
    sx, rx, sy, ry, loc, into, mate_out, mate_in, chain_out, chain_in, skip_out, skip_in, hop_out, hop_in, before, doc_prev, doc_next,
    x_send, x_recv, y_send, y_recv, mate_send, mate_recv, chain_send, chain_recv, skip_send, skip_recv, hop_send, hop_recv, far_send, far_recv,
    doc_send, doc_recv,
):
    me = lax.axis_index("dp")
    pos = lax.axis_index("ctx")
    rows = q_hbm.shape[1]
    pairs = q_hbm.shape[2] // KW
    blocks = rows // BLK
    per = blocks // n_dp
    part = per * BLK
    chips = n_ctx // 2
    has_prev = pos > 0
    has_next = pos < n_ctx - 1
    core = lax.rem(pos, 2)
    own = 1 - core
    mate_pos = pos + 1 - 2 * core
    ahead = 4 * core - 2
    chip = pos // 2
    behind = jnp.where(core == 1, chip, chips - 1 - chip)
    spans = spans_of(n_ctx)

    def has_from(span):
        return behind >= span

    def has_to(span):
        return behind + span < chips

    barrier = pltpu.get_barrier_semaphore()
    for r in range(1, n_dp):
        peer = lax.rem(me + r, n_dp)
        pl.semaphore_signal(barrier, inc=1, device_id={"dp": peer}, device_id_type=MESH)

    peers = n_dp - 1
    for step in (-1, 1, *(sign * 2 * span for span in sorted({1, 2, *spans}) for sign in (-1, 1))):
        there = (pos + step >= 0) & (pos + step < n_ctx)
        peers = peers + there.astype(jnp.int32)

        @pl.when(there)
        def _():
            pl.semaphore_signal(barrier, inc=1, device_id={"ctx": pos + step}, device_id_type=MESH)

    fetches = [
        pltpu.make_async_copy(src, dst, in_sem.at[i])
        for i, (src, dst) in enumerate((
            (order_hbm, order_ref), (doc_hbm, doc_ref), (q_hbm, q_ref), (k_hbm, k_ref), (d_hbm, d_ref),
            (v_hbm, v_ref), (g_hbm, g_ref),
        ))
    ]
    for fetch in fetches:
        fetch.start()

    def my_rows(index):
        return pl.ds(pl.multiple_of(index * part, part), part)

    def lanes(h, width):
        return pl.ds(pl.multiple_of(h * width, width), width)

    for fetch in fetches[:6]:
        fetch.wait()

    order = [order_ref[me, 0, j] for j in range(blocks)]

    def piece(j):
        return slice(j * BLK, (j + 1) * BLK)

    def stage(h, carry):
        for src, width, at in ((q_ref, KW, 0), (k_ref, KW, KW), (d_ref, KW, 2 * KW), (v_ref, VW, 3 * KW)):
            parts = [src[0, piece(j), lanes(h, width)] for j in range(blocks)]
            for dest in range(blocks):
                chosen = parts[0]
                for j in range(1, blocks):
                    chosen = lax.select(order[j] == dest, parts[j], chosen)
                sx[h, piece(dest), at : at + width] = chosen
        return carry

    stage(0, 0)
    pl.semaphore_wait(barrier, peers)

    def exchange(src, dst, send, recv, h, r):
        peer = lax.rem(me + r, n_dp)
        return pltpu.make_async_remote_copy(
            src_ref=src.at[h, my_rows(peer), :],
            dst_ref=dst.at[h, my_rows(me), :],
            send_sem=send.at[h, r],
            recv_sem=recv.at[h, r],
            device_id={"dp": peer},
            device_id_type=MESH,
        )

    def arrival(src, dst, send, recv, h, r):
        source = lax.rem(me + n_dp - r, n_dp)
        return pltpu.make_async_remote_copy(
            src_ref=src.at[h, my_rows(source), :],
            dst_ref=dst.at[h, my_rows(source), :],
            send_sem=send.at[h, r],
            recv_sem=recv.at[h, r],
            device_id={"dp": source},
            device_id_type=MESH,
        )

    def to_ctx(src, dst, send, recv, there):
        return pltpu.make_async_remote_copy(
            src_ref=src, dst_ref=dst, send_sem=send, recv_sem=recv,
            device_id={"ctx": there}, device_id_type=MESH,
        )

    def doc_up():
        return to_ctx(doc_ref, doc_prev, doc_send.at[0], doc_recv.at[0], pos + 1)

    def doc_down():
        return to_ctx(doc_ref, doc_next, doc_send.at[1], doc_recv.at[1], pos - 1)

    def mate(h):
        return to_ctx(mate_out.at[h], mate_in.at[h], mate_send.at[h], mate_recv.at[h], mate_pos)

    def chain(h):
        return to_ctx(chain_out.at[h], chain_in.at[h], chain_send.at[h], chain_recv.at[h], pos + ahead)

    def skip(h):
        return to_ctx(skip_out.at[h], skip_in.at[h], skip_send.at[h], skip_recv.at[h], pos + 2 * ahead)

    def hop(h, i):
        return to_ctx(hop_out.at[i, h], hop_in.at[i, h], hop_send.at[h, i], hop_recv.at[h, i], pos + ahead * spans[i])

    def far(h):
        return to_ctx(before.at[h], into.at[own, h], far_send.at[h], far_recv.at[h], mate_pos)

    def far_arrival(h):
        return to_ctx(before.at[h], into.at[1 - own, h], far_send.at[h], far_recv.at[h], mate_pos)

    def launch(h, carry):
        for r in range(1, n_dp):
            exchange(sx, rx, x_send, x_recv, h, r).start()
        rx[h, my_rows(me), :] = sx[h, my_rows(me), :]
        return carry

    def stage_launch(h, carry):
        stage(h, carry)
        return launch(h, carry)

    launch(0, 0)

    @pl.when(has_next)
    def _():
        doc_up().start()

    @pl.when(has_prev)
    def _():
        doc_down().start()

    lax.fori_loop(1, pairs, stage_launch, 0)

    @pl.when(jnp.logical_not(has_prev))
    def _():
        doc_prev[...] = jnp.full_like(doc_prev, -1)

    @pl.when(jnp.logical_not(has_next))
    def _():
        doc_next[...] = jnp.full_like(doc_next, -1)

    @pl.when(jnp.logical_not(has_from(1)))
    def _():
        chain_in[...] = jnp.zeros_like(chain_in)

    @pl.when(jnp.logical_not(has_from(2)))
    def _():
        skip_in[...] = jnp.zeros_like(skip_in)

    for i, span in enumerate(spans):
        @pl.when(jnp.logical_not(has_from(span)))
        def _():
            hop_in[i] = jnp.zeros_like(hop_in[i])

    fetches[6].wait()

    @pl.when(has_prev)
    def _():
        doc_up().wait_recv()

    @pl.when(has_next)
    def _():
        doc_down().wait_recv()

    doc_row = jnp.broadcast_to(doc_ref[...].astype(F32), (rows, rows))
    doc_col = doc_row.T
    first_row = doc_col[0:1, :]
    last_row = doc_col[rows - 1 : rows, :]
    prev_last = jnp.broadcast_to(doc_prev[:, rows - 1 : rows].astype(F32), (1, rows))
    next_first = jnp.broadcast_to(doc_next[:, 0:1].astype(F32), (1, rows))
    use_state = (prev_last == first_row).astype(F32)
    use_carry = (next_first == last_row).astype(F32)
    single = (first_row == last_row).astype(F32)
    pass_state = single * use_state
    pass_carry = single * use_carry
    pass_own = jnp.where(core == 1, pass_state, pass_carry)
    pass_mate = jnp.where(core == 1, pass_carry, pass_state)
    in_first = (doc_col == first_row).astype(F32)
    in_last = (doc_col == last_row).astype(F32)
    head_w = in_first * use_state
    tail_w = in_last * use_carry
    row_id = lax.broadcasted_iota(jnp.int32, (rows, rows), 0)
    lane_id = lax.broadcasted_iota(jnp.int32, (rows, rows), 1)
    same = (doc_row == doc_col) & (row_id >= lane_id)
    later = ((doc_row == doc_col) & (row_id <= lane_id)).astype(BF16)
    lower = (row_id >= lane_id).astype(BF16)
    in_a = lax.broadcasted_iota(jnp.int32, (rows, KW), 1) < DK
    factor = DK ** (-0.5)

    def load(h):
        q = rx[h, :, 0:KW]
        k = rx[h, :, KW : 2 * KW]
        d = rx[h, :, 2 * KW : 3 * KW]
        v = rx[h, :, 3 * KW : W]
        g = g_ref[0, :, lanes(h, VW)]
        cum = dot(lower, d, NN)
        total = cum[rows - 1 : rows, :]
        growth = jnp.exp(cum)
        shrink = jnp.exp(-cum)
        to_end = jnp.exp(total - cum)
        grow[h] = growth
        end[h] = to_end
        return q.astype(F32), k.astype(F32), v, g, d, growth, shrink, to_end, jnp.exp(total)

    def fold(wide):
        return jnp.concatenate([wide[0:DK, 0:DV], wide[DK:KW, DV:VW]], axis=0)

    def spread(tall):
        nil = jnp.zeros((DK, DV), tall.dtype)
        top = jnp.concatenate([tall[0:DK], nil], axis=1)
        low = jnp.concatenate([nil, tall[DK:KW]], axis=1)
        return jnp.concatenate([top, low], axis=0)

    def nearby(h):
        for r in range(1, n_dp):
            arrival(sx, rx, x_send, x_recv, h, r).wait_recv()
        q_f, k_f, v, g, d, growth, shrink, to_end, fade = load(h)
        loc[0, h] = fold(dot(split(k_f * to_end * in_last), v, TN))
        loc[1, h] = factor * fold(dot(split(q_f * growth * in_first), g, TN))
        decay[h] = jnp.exp(dot(d, jnp.ones((rows, DV), BF16), TN))
        mate_out[h, 0:KW] = loc[1 - own, h]
        mate_out[h, KW : 2 * KW] = pass_mate * decay[h]
        mate_out[h, 2 * KW : 2 * KW + TILE] = jnp.broadcast_to(pass_mate * fade, (TILE, KW))
        chain_out[h, KW : KW + TILE] = jnp.broadcast_to(pass_own * fade, (TILE, KW))
        mate(h).start()
        q_t = q_f * growth
        k_t = k_f * shrink
        zero = jnp.zeros_like(q_t)
        q_2 = split(jnp.concatenate([jnp.where(in_a, q_t, zero), jnp.where(in_a, zero, q_t)], axis=0))
        k_s = split(k_t)
        k_2 = split(jnp.concatenate([jnp.where(in_a, k_t, zero), jnp.where(in_a, zero, k_t)], axis=0))
        same_2 = jnp.concatenate([same, same], axis=0)
        score_2 = split(jnp.where(same_2, dot(q_2, k_s, NT), 0.0))
        v_a, v_b = v[:, 0:DV], v[:, DV:VW]
        g_a, g_b = g[:, 0:DV], g[:, DV:VW]
        score_a = both(lambda x: x[0:rows], score_2)
        score_b = both(lambda x: x[rows : 2 * rows], score_2)
        near[h, :, 0:DV] = dot(score_a, v_a, NN)
        near[h, :, DV:VW] = dot(score_b, v_b, NN)
        dv_near[h, :, 0:DV] = dot(score_a, g_a, TN)
        dv_near[h, :, DV:VW] = dot(score_b, g_b, TN)
        gs_a = jnp.where(same, dot(g_a, v_a, NT), 0.0)
        gs_b = jnp.where(same, dot(g_b, v_b, NT), 0.0)
        dq_near[h] = dot(split(jnp.concatenate([gs_a, gs_b], axis=1)), k_2, NN)
        dk_near[h] = factor * shrink * dot(split(jnp.concatenate([gs_a, gs_b], axis=0)), q_2, TN)

    def finish(h):
        far_arrival(h).wait_recv()
        q_f = rx[h, :, 0:KW].astype(F32)
        k_f = rx[h, :, KW : 2 * KW].astype(F32)
        v = rx[h, :, 3 * KW : W]
        g = g_ref[0, :, lanes(h, VW)]
        growth = grow[h]
        to_end = end[h]
        q_t = q_f * growth
        k_e = k_f * to_end * tail_w
        f_in = into[0, h]
        b_in = into[1, h]
        f_end = loc[0, h] + pass_state * decay[h] * f_in
        state = both(spread, split(f_in))
        carry = both(spread, split(b_in))
        far = dot(split(q_t * head_w), state, NN)
        out_ref[0, :, lanes(h, VW)] = (factor * (near[h] + far)).astype(BF16)
        dq = factor * growth * (dq_near[h] + dot(g, state, NT) * head_w)
        dk = dk_near[h] + to_end * dot(v, carry, NT) * tail_w
        dv = factor * dv_near[h] + dot(split(k_e), carry, NN)
        log_grad = q_f * dq - k_f * dk
        sums = dot(jnp.ones((8, DV), BF16), split(f_end * b_in), NT)
        dd = dot(later, split(log_grad), NN) + sums[0:1] * tail_w
        sy[h, :, 0:KW] = dq.astype(BF16)
        sy[h, :, KW : 2 * KW] = dk.astype(BF16)
        sy[h, :, 2 * KW : 3 * KW] = dd.astype(BF16)
        sy[h, :, 3 * KW : W] = dv.astype(BF16)
        ry[h, my_rows(me), :] = sy[h, my_rows(me), :]
        for r in range(1, n_dp):
            exchange(sy, ry, y_send, y_recv, h, r).start()

    def column(tile):
        return jnp.broadcast_to(tile[0:1], (DV, KW)).T

    def depart(h):
        mate(h).wait_recv()
        chain_out[h, 0:KW] = loc[own, h] + pass_own * decay[h] * mate_in[h, 0:KW]
        chain_out[h, KW : KW + TILE] = chain_out[h, KW : KW + TILE] * mate_in[h, 2 * KW : 2 * KW + TILE]

        @pl.when(has_to(1))
        def _():
            chain(h).start()

        @pl.when(has_to(2))
        def _():
            skip_out[h] = chain_out[h, 0 : skip_out.shape[1]].astype(skip_out.dtype)
            skip(h).start()

    def join(h, near_ref, far_ref, i):
        fade = near_ref[KW : KW + TILE]
        state = near_ref[0:KW] + column(fade) * far_ref[0:KW].astype(F32)
        if i < len(spans):
            hop_out[i, h, 0:KW] = state
            hop_out[i, h, KW : KW + TILE] = fade * far_ref[KW : KW + TILE]

            @pl.when(has_to(spans[i]))
            def _():
                hop(h, i).start()
        else:
            before[h] = state
            far(h).start()
            into[own, h] = mate_in[h, 0:KW] + mate_in[h, KW : 2 * KW] * state

    def arrive(h):
        @pl.when(has_from(1))
        def _():
            chain(h).wait_recv()

        @pl.when(has_from(2))
        def _():
            skip(h).wait_recv()

        join(h, chain_in.at[h], skip_in.at[h], 0)

    def widen(h, i):
        @pl.when(has_from(spans[i]))
        def _():
            hop(h, i).wait_recv()
        join(h, hop_out.at[i, h], hop_in.at[i, h], i + 1)

    stages = [(0, nearby), (0, depart), (FLIGHT, arrive)]
    for i in range(len(spans)):
        stages.append(((i + 2) * FLIGHT, functools.partial(widen, i=i)))
    last = stages[-1][0] + 1
    stages.insert(1, (last, finish))

    def step(t, carry):
        for lag, stage_of in stages:
            @pl.when((t >= lag) & (t < lag + pairs))
            def _():
                stage_of(t - lag)

        return carry

    lax.fori_loop(0, last + pairs, step, 0)

    @pl.when(has_next)
    def _():
        doc_up().wait_send()

    @pl.when(has_prev)
    def _():
        doc_down().wait_send()

    def home(h, carry):
        mate(h).wait_send()
        far(h).wait_send()

        @pl.when(has_to(1))
        def _():
            chain(h).wait_send()

        @pl.when(has_to(2))
        def _():
            skip(h).wait_send()

        for i, span in enumerate(spans):
            @pl.when(has_to(span))
            def _():
                hop(h, i).wait_send()
        for r in range(1, n_dp):
            exchange(sx, rx, x_send, x_recv, h, r).wait_send()
            exchange(sy, ry, y_send, y_recv, h, r).wait_send()
        for r in range(1, n_dp):
            arrival(sy, ry, y_send, y_recv, h, r).wait_recv()
        for dst, width, at in ((dq_ref, KW, 0), (dk_ref, KW, KW), (dd_ref, KW, 2 * KW), (dv_ref, VW, 3 * KW)):
            parts = [ry[h, piece(j), at : at + width] for j in range(blocks)]
            for j in range(blocks):
                chosen = parts[0]
                for source in range(1, blocks):
                    chosen = lax.select(order[j] == source, parts[source], chosen)
                dst[0, piece(j), lanes(h, width)] = chosen
        return carry

    lax.fori_loop(0, pairs, home, 0)


def store(*refs):
    half = len(refs) // 2
    sem = refs[-1]
    copies = [pltpu.make_async_copy(refs[i], refs[half + i], sem.at[i]) for i in range(half)]
    for copy in copies:
        copy.start()
    for copy in copies:
        copy.wait()


def spans_of(n_ctx):
    chips = n_ctx // 2
    span, spans = 2, []
    while span < chips // 2:
        spans.append(span)
        span *= 2
    return spans


def body(n_dp, n_ctx, query_rows, key_rows, value_rows, log_decay, out_grad, doc_ids, block_order):
    rows, hk = query_rows.shape[1:]
    hv = value_rows.shape[2]
    pairs = hk // KW
    rounds = max(len(spans_of(n_ctx)), 1)
    skipped = pltpu.VMEM((pairs, KW + TILE, DV), F32) if spans_of(n_ctx) else pltpu.VMEM((pairs, KW, DV), BF16)
    vmem = pl.BlockSpec(memory_space=pltpu.VMEM)
    keys = jax.ShapeDtypeStruct((1, rows, hk), BF16)
    values = jax.ShapeDtypeStruct((1, rows, hv), BF16)
    outs = (values, keys, keys, values, keys)
    dma = pltpu.SemaphoreType.DMA
    held = pl.pallas_call(
        functools.partial(kernel, n_dp, n_ctx),
        out_shape=tuple(pltpu.VMEM(x.shape, BF16) for x in outs),
        in_specs=[pl.BlockSpec(memory_space=pltpu.HBM)] * 7,
        out_specs=(vmem,) * 5,
        scratch_shapes=[
            pltpu.SMEM(block_order.shape, jnp.int32),
            pltpu.VMEM((1, rows), jnp.int32),
            pltpu.VMEM((1, rows, hk), BF16),
            pltpu.VMEM((1, rows, hk), BF16),
            pltpu.VMEM((1, rows, hv), BF16),
            pltpu.VMEM((1, rows, hk), BF16),
            pltpu.VMEM((1, rows, hv), BF16),
            dma((7,)),
            pltpu.VMEM((pairs, KW, DV), F32),
            pltpu.VMEM((pairs, rows, KW), F32),
            pltpu.VMEM((pairs, rows, KW), F32),
            pltpu.VMEM((pairs, rows, VW), F32),
            pltpu.VMEM((pairs, rows, VW), F32),
            pltpu.VMEM((pairs, rows, KW), F32),
            pltpu.VMEM((pairs, rows, KW), F32),
            pltpu.VMEM((pairs, rows, W), BF16),
            pltpu.VMEM((pairs, rows, W), BF16),
            pltpu.VMEM((pairs, rows, W), BF16),
            pltpu.VMEM((pairs, rows, W), BF16),
            pltpu.VMEM((2, pairs, KW, DV), F32),
            pltpu.VMEM((2, pairs, KW, DV), F32),
            pltpu.VMEM((pairs, 2 * KW + TILE, DV), F32),
            pltpu.VMEM((pairs, 2 * KW + TILE, DV), F32),
            pltpu.VMEM((pairs, KW + TILE, DV), F32),
            pltpu.VMEM((pairs, KW + TILE, DV), F32),
            skipped, skipped,
            pltpu.VMEM((rounds, pairs, KW + TILE, DV), F32),
            pltpu.VMEM((rounds, pairs, KW + TILE, DV), F32),
            pltpu.VMEM((pairs, KW, DV), F32),
            pltpu.VMEM((1, rows), jnp.int32),
            pltpu.VMEM((1, rows), jnp.int32),
            dma((pairs, n_dp)), dma((pairs, n_dp)), dma((pairs, n_dp)), dma((pairs, n_dp)),
            dma((pairs,)), dma((pairs,)), dma((pairs,)), dma((pairs,)), dma((pairs,)), dma((pairs,)), dma((pairs, rounds)), dma((pairs, rounds)),
            dma((pairs,)), dma((pairs,)),
            dma((2,)), dma((2,)),
        ],
        compiler_params=pltpu.CompilerParams(
            collective_id=0, has_side_effects=True, vmem_limit_bytes=56 * 1024 * 1024
        ),
    )(block_order, doc_ids, query_rows, key_rows, value_rows, log_decay, out_grad)
    return pl.pallas_call(
        store,
        out_shape=outs,
        in_specs=(vmem,) * 5,
        out_specs=(pl.BlockSpec(memory_space=pltpu.HBM),) * 5,
        scratch_shapes=[dma((5,))],
    )(*(pltpu.with_memory_space_constraint(x, pltpu.VMEM) for x in held))


def solution(mesh):
    placed = P("dp", "ctx", None)
    return jax.shard_map(
        functools.partial(body, mesh.shape["dp"], mesh.shape["ctx"]),
        mesh=mesh,
        in_specs=(placed,) * 5 + (P("dp", "ctx"), P(None, "ctx", None)),
        out_specs=(placed,) * 5,
        check_vma=False,
    )
```

```python
import functools

import jax
import jax.numpy as jnp
from jax import lax
from jax.experimental import pallas as pl
from jax.experimental.pallas import tpu as pltpu
from jax.sharding import PartitionSpec as P

DK = 64
DV = 128
BLK = 32
KW = 2 * DK
VW = 2 * DV
W = 3 * KW + VW
TILE = 8
FLIGHT = 2
FAR_FLIGHT = 3
MESH = pl.DeviceIdType.MESH
F32 = jnp.float32
BF16 = jnp.bfloat16

NN = (((1,), (0,)), ((), ()))
NT = (((1,), (1,)), ((), ()))
TN = (((0,), (0,)), ((), ()))


def split(x):
    hi = x.astype(BF16)
    return hi, (x - hi.astype(F32)).astype(BF16)


def dot(a, b, dims):
    a = a if isinstance(a, tuple) else (a,)
    b = b if isinstance(b, tuple) else (b,)
    total = None
    for i, left in enumerate(a):
        for j, right in enumerate(b):
            if i + j > 1:
                continue
            term = lax.dot_general(left, right, dims, preferred_element_type=F32)
            total = term if total is None else total + term
    return total


def both(fn, pair):
    return tuple(fn(x) for x in pair)


def kernel(
    n_dp, n_ctx, order_hbm, doc_hbm, q_hbm, k_hbm, v_hbm, d_hbm, g_hbm,
    out_ref, dq_ref, dk_ref, dv_ref, dd_ref,
    order_ref, doc_ref, q_ref, k_ref, v_ref, d_ref, g_ref, in_sem, decay, grow, end, near, dv_near, dq_near, dk_near,
    sx, rx, sy, ry, loc, into, mate_out, mate_in, chain_out, relay_out, chain_in, hop_out, hop_in, before, doc_prev, doc_next,
    x_send, x_recv, y_send, y_recv, mate_send, mate_recv, chain_send, chain_recv, hop_send, hop_recv, far_send, far_recv,
    doc_send, doc_recv,
):
    me = lax.axis_index("dp")
    pos = lax.axis_index("ctx")
    rows = q_hbm.shape[1]
    pairs = q_hbm.shape[2] // KW
    blocks = rows // BLK
    per = blocks // n_dp
    part = per * BLK
    chips = n_ctx // 2
    has_prev = pos > 0
    has_next = pos < n_ctx - 1
    core = lax.rem(pos, 2)
    own = 1 - core
    mate_pos = pos + 1 - 2 * core
    ahead = 4 * core - 2
    chip = pos // 2
    behind = jnp.where(core == 1, chip, chips - 1 - chip)
    second = behind == 1
    third = behind == 2
    spans = spans_of(n_ctx)

    def has_from(span):
        return behind >= span

    def has_to(span):
        return behind + span < chips

    barrier = pltpu.get_barrier_semaphore()
    for r in range(1, n_dp):
        peer = lax.rem(me + r, n_dp)
        pl.semaphore_signal(barrier, inc=1, device_id={"dp": peer}, device_id_type=MESH)

    peers = n_dp - 1
    for step in (-1, 1, *(sign * 2 * span for span in sorted({1, 2, *spans}) for sign in (-1, 1))):
        there = (pos + step >= 0) & (pos + step < n_ctx)
        peers = peers + there.astype(jnp.int32)

        @pl.when(there)
        def _():
            pl.semaphore_signal(barrier, inc=1, device_id={"ctx": pos + step}, device_id_type=MESH)

    fetches = [
        pltpu.make_async_copy(src, dst, in_sem.at[i])
        for i, (src, dst) in enumerate((
            (order_hbm, order_ref), (q_hbm, q_ref), (k_hbm, k_ref), (d_hbm, d_ref),
            (v_hbm, v_ref), (doc_hbm, doc_ref), (g_hbm, g_ref),
        ))
    ]
    for fetch in fetches:
        fetch.start()

    def my_rows(index):
        return pl.ds(pl.multiple_of(index * part, part), part)

    def lanes(h, width):
        return pl.ds(pl.multiple_of(h * width, width), width)

    for fetch in fetches[:5]:
        fetch.wait()

    @pl.when(jnp.logical_not(has_prev))
    def _():
        doc_prev[...] = jnp.full_like(doc_prev, -1)

    @pl.when(jnp.logical_not(has_next))
    def _():
        doc_next[...] = jnp.full_like(doc_next, -1)

    for span in (1, 2):
        @pl.when(jnp.logical_not(has_from(span)))
        def _():
            chain_in[span - 1] = jnp.zeros_like(chain_in[span - 1])

    @pl.when(third)
    def _():
        chain_in[1] = jnp.zeros_like(chain_in[1])

    for i, span in enumerate(spans):
        @pl.when(jnp.logical_not(has_from(span)))
        def _():
            hop_in[i] = jnp.zeros_like(hop_in[i])

    order = [order_ref[me, 0, j] for j in range(blocks)]

    def piece(j):
        return slice(j * BLK, (j + 1) * BLK)

    def stage(h, carry):
        for src, width, at in ((q_ref, KW, 0), (k_ref, KW, KW), (d_ref, KW, 2 * KW), (v_ref, VW, 3 * KW)):
            parts = [src[0, piece(j), lanes(h, width)] for j in range(blocks)]
            for dest in range(blocks):
                chosen = parts[0]
                for j in range(1, blocks):
                    chosen = lax.select(order[j] == dest, parts[j], chosen)
                sx[h, piece(dest), at : at + width] = chosen
        return carry

    lax.fori_loop(0, pairs, stage, 0)

    pl.semaphore_wait(barrier, peers)

    def exchange(src, dst, send, recv, h, r):
        peer = lax.rem(me + r, n_dp)
        return pltpu.make_async_remote_copy(
            src_ref=src.at[h, my_rows(peer), :],
            dst_ref=dst.at[h, my_rows(me), :],
            send_sem=send.at[h, r],
            recv_sem=recv.at[h, r],
            device_id={"dp": peer},
            device_id_type=MESH,
        )

    def arrival(src, dst, send, recv, h, r):
        source = lax.rem(me + n_dp - r, n_dp)
        return pltpu.make_async_remote_copy(
            src_ref=src.at[h, my_rows(source), :],
            dst_ref=dst.at[h, my_rows(source), :],
            send_sem=send.at[h, r],
            recv_sem=recv.at[h, r],
            device_id={"dp": source},
            device_id_type=MESH,
        )

    def to_ctx(src, dst, send, recv, there):
        return pltpu.make_async_remote_copy(
            src_ref=src, dst_ref=dst, send_sem=send, recv_sem=recv,
            device_id={"ctx": there}, device_id_type=MESH,
        )

    def doc_up():
        return to_ctx(doc_ref, doc_prev, doc_send.at[0], doc_recv.at[0], pos + 1)

    def doc_down():
        return to_ctx(doc_ref, doc_next, doc_send.at[1], doc_recv.at[1], pos - 1)

    def mate(h):
        return to_ctx(mate_out.at[h], mate_in.at[h], mate_send.at[h], mate_recv.at[h], mate_pos)

    def chain(h, span):
        size = KW + TILE if span == 1 or spans else KW
        return to_ctx(
            chain_out.at[h, 0:size], chain_in.at[span - 1, h, 0:size],
            chain_send.at[h, span - 1], chain_recv.at[h, span - 1], pos + ahead * span,
        )

    def relay(h):
        return to_ctx(
            relay_out.at[h], chain_in.at[0, h], chain_send.at[h, 0], chain_recv.at[h, 0], pos + ahead,
        )

    sends_near = has_to(1) & jnp.logical_not(second)
    sends_far = has_to(2) & (behind > 0)
    relays = has_to(1) & second

    def hop(h, i):
        return to_ctx(hop_out.at[i, h], hop_in.at[i, h], hop_send.at[h, i], hop_recv.at[h, i], pos + ahead * spans[i])

    def far(h):
        return to_ctx(before.at[h], into.at[own, h], far_send.at[h], far_recv.at[h], mate_pos)

    def far_arrival(h):
        return to_ctx(before.at[h], into.at[1 - own, h], far_send.at[h], far_recv.at[h], mate_pos)

    def launch(h, carry):
        for r in range(1, n_dp):
            exchange(sx, rx, x_send, x_recv, h, r).start()
        rx[h, my_rows(me), :] = sx[h, my_rows(me), :]
        return carry

    lax.fori_loop(0, pairs, launch, 0)

    for fetch in fetches[5:]:
        fetch.wait()

    @pl.when(has_next)
    def _():
        doc_up().start()

    @pl.when(has_prev)
    def _():
        doc_down().start()

    @pl.when(has_prev)
    def _():
        doc_up().wait_recv()

    @pl.when(has_next)
    def _():
        doc_down().wait_recv()

    doc_row = jnp.broadcast_to(doc_ref[...].astype(F32), (rows, rows))
    doc_col = doc_row.T
    first_row = doc_col[0:1, :]
    last_row = doc_col[rows - 1 : rows, :]
    prev_last = jnp.broadcast_to(doc_prev[:, rows - 1 : rows].astype(F32), (1, rows))
    next_first = jnp.broadcast_to(doc_next[:, 0:1].astype(F32), (1, rows))
    use_state = (prev_last == first_row).astype(F32)
    use_carry = (next_first == last_row).astype(F32)
    single = (first_row == last_row).astype(F32)
    pass_state = single * use_state
    pass_carry = single * use_carry
    pass_own = jnp.where(core == 1, pass_state, pass_carry)
    pass_mate = jnp.where(core == 1, pass_carry, pass_state)
    in_first = (doc_col == first_row).astype(F32)
    in_last = (doc_col == last_row).astype(F32)
    head_w = in_first * use_state
    tail_w = in_last * use_carry
    row_id = lax.broadcasted_iota(jnp.int32, (rows, rows), 0)
    lane_id = lax.broadcasted_iota(jnp.int32, (rows, rows), 1)
    same = (doc_row == doc_col) & (row_id >= lane_id)
    later = ((doc_row == doc_col) & (row_id <= lane_id)).astype(BF16)
    lower = (row_id >= lane_id).astype(BF16)
    in_a = lax.broadcasted_iota(jnp.int32, (rows, KW), 1) < DK
    factor = DK ** (-0.5)

    def load(h):
        q = rx[h, :, 0:KW]
        k = rx[h, :, KW : 2 * KW]
        d = rx[h, :, 2 * KW : 3 * KW]
        v = rx[h, :, 3 * KW : W]
        g = g_ref[0, :, lanes(h, VW)]
        cum = dot(lower, d, NN)
        total = cum[rows - 1 : rows, :]
        growth = jnp.exp(cum)
        shrink = jnp.exp(-cum)
        to_end = jnp.exp(total - cum)
        grow[h] = growth
        end[h] = to_end
        return q.astype(F32), k.astype(F32), v, g, d, growth, shrink, to_end, jnp.exp(total)

    def fold(wide):
        return jnp.concatenate([wide[0:DK, 0:DV], wide[DK:KW, DV:VW]], axis=0)

    def spread(tall):
        nil = jnp.zeros((DK, DV), tall.dtype)
        top = jnp.concatenate([tall[0:DK], nil], axis=1)
        low = jnp.concatenate([nil, tall[DK:KW]], axis=1)
        return jnp.concatenate([top, low], axis=0)

    def nearby(h):
        for r in range(1, n_dp):
            arrival(sx, rx, x_send, x_recv, h, r).wait_recv()
        q_f, k_f, v, g, d, growth, shrink, to_end, fade = load(h)
        loc[0, h] = fold(dot(split(k_f * to_end * in_last), v, TN))
        loc[1, h] = factor * fold(dot(split(q_f * growth * in_first), g, TN))
        decay[h] = jnp.exp(dot(d, jnp.ones((rows, DV), BF16), TN))
        mate_out[h, 0:KW] = loc[1 - own, h]
        mate_out[h, KW : 2 * KW] = pass_mate * decay[h]
        mate_out[h, 2 * KW : 2 * KW + TILE] = jnp.broadcast_to(pass_mate * fade, (TILE, KW))
        chain_out[h, KW : KW + TILE] = jnp.broadcast_to(pass_own * fade, (TILE, KW))
        mate(h).start()
        q_t = q_f * growth
        k_t = k_f * shrink
        zero = jnp.zeros_like(q_t)
        q_2 = split(jnp.concatenate([jnp.where(in_a, q_t, zero), jnp.where(in_a, zero, q_t)], axis=0))
        k_s = split(k_t)
        k_2 = split(jnp.concatenate([jnp.where(in_a, k_t, zero), jnp.where(in_a, zero, k_t)], axis=0))
        same_2 = jnp.concatenate([same, same], axis=0)
        score_2 = split(jnp.where(same_2, dot(q_2, k_s, NT), 0.0))
        v_a, v_b = v[:, 0:DV], v[:, DV:VW]
        g_a, g_b = g[:, 0:DV], g[:, DV:VW]
        score_a = both(lambda x: x[0:rows], score_2)
        score_b = both(lambda x: x[rows : 2 * rows], score_2)
        near[h, :, 0:DV] = dot(score_a, v_a, NN)
        near[h, :, DV:VW] = dot(score_b, v_b, NN)
        dv_near[h, :, 0:DV] = dot(score_a, g_a, TN)
        dv_near[h, :, DV:VW] = dot(score_b, g_b, TN)
        gs_a = jnp.where(same, dot(g_a, v_a, NT), 0.0)
        gs_b = jnp.where(same, dot(g_b, v_b, NT), 0.0)
        dq_near[h] = dot(split(jnp.concatenate([gs_a, gs_b], axis=1)), k_2, NN)
        dk_near[h] = factor * shrink * dot(split(jnp.concatenate([gs_a, gs_b], axis=0)), q_2, TN)

    def finish(h):
        far_arrival(h).wait_recv()
        q_f = rx[h, :, 0:KW].astype(F32)
        k_f = rx[h, :, KW : 2 * KW].astype(F32)
        v = rx[h, :, 3 * KW : W]
        g = g_ref[0, :, lanes(h, VW)]
        growth = grow[h]
        to_end = end[h]
        q_t = q_f * growth
        k_e = k_f * to_end * tail_w
        f_in = into[0, h]
        b_in = into[1, h]
        f_end = loc[0, h] + pass_state * decay[h] * f_in
        state = both(spread, split(f_in))
        carry = both(spread, split(b_in))
        far = dot(split(q_t * head_w), state, NN)
        out_ref[0, :, lanes(h, VW)] = (factor * (near[h] + far)).astype(BF16)
        dq = factor * growth * (dq_near[h] + dot(g, state, NT) * head_w)
        dk = dk_near[h] + to_end * dot(v, carry, NT) * tail_w
        dv = factor * dv_near[h] + dot(split(k_e), carry, NN)
        log_grad = q_f * dq - k_f * dk
        sums = dot(jnp.ones((8, DV), BF16), split(f_end * b_in), NT)
        dd = dot(later, split(log_grad), NN) + sums[0:1] * tail_w
        sy[h, :, 0:KW] = dq.astype(BF16)
        sy[h, :, KW : 2 * KW] = dk.astype(BF16)
        sy[h, :, 2 * KW : 3 * KW] = dd.astype(BF16)
        sy[h, :, 3 * KW : W] = dv.astype(BF16)
        ry[h, my_rows(me), :] = sy[h, my_rows(me), :]
        for r in range(1, n_dp):
            exchange(sy, ry, y_send, y_recv, h, r).start()

    def column(tile):
        return jnp.broadcast_to(tile[0:1], (DV, KW)).T

    def depart(h):
        mate(h).wait_recv()
        chain_out[h, 0:KW] = loc[own, h] + pass_own * decay[h] * mate_in[h, 0:KW]
        chain_out[h, KW : KW + TILE] = chain_out[h, KW : KW + TILE] * mate_in[h, 2 * KW : 2 * KW + TILE]

        @pl.when(sends_near)
        def _():
            chain(h, 1).start()

        @pl.when(sends_far)
        def _():
            chain(h, 2).start()

    def join(h, near_ref, far_ref, i):
        fade = near_ref[KW : KW + TILE]
        state = near_ref[0:KW] + column(fade) * far_ref[0:KW]
        if i < len(spans):
            hop_out[i, h, 0:KW] = state
            hop_out[i, h, KW : KW + TILE] = fade * far_ref[KW : KW + TILE]

            @pl.when(has_to(spans[i]))
            def _():
                hop(h, i).start()
        else:
            before[h] = state
            far(h).start()
            into[own, h] = mate_in[h, 0:KW] + mate_in[h, KW : 2 * KW] * state

    def arrive(h):
        @pl.when(has_from(1))
        def _():
            chain(h, 1).wait_recv()

        @pl.when(has_from(3))
        def _():
            chain(h, 2).wait_recv()

        @pl.when(relays)
        def _():
            fade = chain_out[h, KW : KW + TILE]
            relay_out[h, 0:KW] = chain_out[h, 0:KW] + column(fade) * chain_in[0, h, 0:KW]
            relay_out[h, KW : KW + TILE] = fade
            relay(h).start()

        join(h, chain_in.at[0, h], chain_in.at[1, h], 0)

    def widen(h, i):
        @pl.when(has_from(spans[i]))
        def _():
            hop(h, i).wait_recv()
        join(h, hop_out.at[i, h], hop_in.at[i, h], i + 1)

    def flight(place):
        return jnp.where(place == 2, 2 * FLIGHT, jnp.where(place > 2, FAR_FLIGHT, FLIGHT))

    stages = [(0, nearby), (0, depart), (flight(behind), arrive)]
    last = max(2 * FLIGHT, FAR_FLIGHT) + 1
    for i in range(len(spans)):
        stages.append((last + i * FAR_FLIGHT, functools.partial(widen, i=i)))
    if spans:
        last += len(spans) * FAR_FLIGHT
        stages.insert(1, (last, finish))
    else:
        stages.insert(1, (jnp.maximum(flight(behind), flight(chips - 1 - behind)) + 1, finish))

    def step(t, carry):
        for lag, stage_of in stages:
            @pl.when((t >= lag) & (t < lag + pairs))
            def _():
                stage_of(t - lag)

        return carry

    lax.fori_loop(0, last + pairs, step, 0)

    @pl.when(has_next)
    def _():
        doc_up().wait_send()

    @pl.when(has_prev)
    def _():
        doc_down().wait_send()

    def home(h, carry):
        mate(h).wait_send()
        far(h).wait_send()

        @pl.when(has_to(1))
        def _():
            chain(h, 1).wait_send()

        @pl.when(sends_far)
        def _():
            chain(h, 2).wait_send()

        for i, span in enumerate(spans):
            @pl.when(has_to(span))
            def _():
                hop(h, i).wait_send()
        for r in range(1, n_dp):
            exchange(sx, rx, x_send, x_recv, h, r).wait_send()
            exchange(sy, ry, y_send, y_recv, h, r).wait_send()
        for r in range(1, n_dp):
            arrival(sy, ry, y_send, y_recv, h, r).wait_recv()
        for dst, width, at in ((dq_ref, KW, 0), (dk_ref, KW, KW), (dd_ref, KW, 2 * KW), (dv_ref, VW, 3 * KW)):
            parts = [ry[h, piece(j), at : at + width] for j in range(blocks)]
            for j in range(blocks):
                chosen = parts[0]
                for source in range(1, blocks):
                    chosen = lax.select(order[j] == source, parts[source], chosen)
                dst[0, piece(j), lanes(h, width)] = chosen
        return carry

    lax.fori_loop(0, pairs, home, 0)


def store(*refs):
    half = len(refs) // 2
    sem = refs[-1]
    copies = [pltpu.make_async_copy(refs[i], refs[half + i], sem.at[i]) for i in range(half)]
    for copy in copies:
        copy.start()
    for copy in copies:
        copy.wait()


def spans_of(n_ctx):
    chips = n_ctx // 2
    span, spans = 2, []
    while span < chips // 2:
        spans.append(span)
        span *= 2
    return spans


def body(n_dp, n_ctx, query_rows, key_rows, value_rows, log_decay, out_grad, doc_ids, block_order):
    rows, hk = query_rows.shape[1:]
    hv = value_rows.shape[2]
    pairs = hk // KW
    rounds = max(len(spans_of(n_ctx)), 1)
    vmem = pl.BlockSpec(memory_space=pltpu.VMEM)
    keys = jax.ShapeDtypeStruct((1, rows, hk), BF16)
    values = jax.ShapeDtypeStruct((1, rows, hv), BF16)
    outs = (values, keys, keys, values, keys)
    dma = pltpu.SemaphoreType.DMA
    held = pl.pallas_call(
        functools.partial(kernel, n_dp, n_ctx),
        out_shape=tuple(pltpu.VMEM(x.shape, BF16) for x in outs),
        in_specs=[pl.BlockSpec(memory_space=pltpu.HBM)] * 7,
        out_specs=(vmem,) * 5,
        scratch_shapes=[
            pltpu.SMEM(block_order.shape, jnp.int32),
            pltpu.VMEM((1, rows), jnp.int32),
            pltpu.VMEM((1, rows, hk), BF16),
            pltpu.VMEM((1, rows, hk), BF16),
            pltpu.VMEM((1, rows, hv), BF16),
            pltpu.VMEM((1, rows, hk), BF16),
            pltpu.VMEM((1, rows, hv), BF16),
            dma((7,)),
            pltpu.VMEM((pairs, KW, DV), F32),
            pltpu.VMEM((pairs, rows, KW), F32),
            pltpu.VMEM((pairs, rows, KW), F32),
            pltpu.VMEM((pairs, rows, VW), F32),
            pltpu.VMEM((pairs, rows, VW), F32),
            pltpu.VMEM((pairs, rows, KW), F32),
            pltpu.VMEM((pairs, rows, KW), F32),
            pltpu.VMEM((pairs, rows, W), BF16),
            pltpu.VMEM((pairs, rows, W), BF16),
            pltpu.VMEM((pairs, rows, W), BF16),
            pltpu.VMEM((pairs, rows, W), BF16),
            pltpu.VMEM((2, pairs, KW, DV), F32),
            pltpu.VMEM((2, pairs, KW, DV), F32),
            pltpu.VMEM((pairs, 2 * KW + TILE, DV), F32),
            pltpu.VMEM((pairs, 2 * KW + TILE, DV), F32),
            pltpu.VMEM((pairs, KW + TILE, DV), F32),
            pltpu.VMEM((pairs, KW + TILE, DV), F32),
            pltpu.VMEM((2, pairs, KW + TILE, DV), F32),
            pltpu.VMEM((rounds, pairs, KW + TILE, DV), F32),
            pltpu.VMEM((rounds, pairs, KW + TILE, DV), F32),
            pltpu.VMEM((pairs, KW, DV), F32),
            pltpu.VMEM((1, rows), jnp.int32),
            pltpu.VMEM((1, rows), jnp.int32),
            dma((pairs, n_dp)), dma((pairs, n_dp)), dma((pairs, n_dp)), dma((pairs, n_dp)),
            dma((pairs,)), dma((pairs,)), dma((pairs, 2)), dma((pairs, 2)), dma((pairs, rounds)), dma((pairs, rounds)),
            dma((pairs,)), dma((pairs,)),
            dma((2,)), dma((2,)),
        ],
        compiler_params=pltpu.CompilerParams(
            collective_id=0, has_side_effects=True, vmem_limit_bytes=56 * 1024 * 1024
        ),
    )(block_order, doc_ids, query_rows, key_rows, value_rows, log_decay, out_grad)
    return pl.pallas_call(
        store,
        out_shape=outs,
        in_specs=(vmem,) * 5,
        out_specs=(pl.BlockSpec(memory_space=pltpu.HBM),) * 5,
        scratch_shapes=[dma((5,))],
    )(*(pltpu.with_memory_space_constraint(x, pltpu.VMEM) for x in held))


def solution(mesh):
    placed = P("dp", "ctx", None)
    return jax.shard_map(
        functools.partial(body, mesh.shape["dp"], mesh.shape["ctx"]),
        mesh=mesh,
        in_specs=(placed,) * 5 + (P("dp", "ctx"), P(None, "ctx", None)),
        out_specs=(placed,) * 5,
        check_vma=False,
    )
```

```python
import functools

import jax
import jax.numpy as jnp
from jax import lax
from jax.experimental import pallas as pl
from jax.experimental.pallas import tpu as pltpu
from jax.sharding import PartitionSpec as P

DK = 64
DV = 128
BLK = 32
KW = 2 * DK
VW = 2 * DV
W = 3 * KW + VW
TILE = 8
FLIGHT = 2
FAR_FLIGHT = 3
MESH = pl.DeviceIdType.MESH
F32 = jnp.float32
BF16 = jnp.bfloat16

NN = (((1,), (0,)), ((), ()))
NT = (((1,), (1,)), ((), ()))
TN = (((0,), (0,)), ((), ()))


def split(x):
    hi = x.astype(BF16)
    return hi, (x - hi.astype(F32)).astype(BF16)


def dot(a, b, dims):
    a = a if isinstance(a, tuple) else (a,)
    b = b if isinstance(b, tuple) else (b,)
    total = None
    for i, left in enumerate(a):
        for j, right in enumerate(b):
            if i + j > 1:
                continue
            term = lax.dot_general(left, right, dims, preferred_element_type=F32)
            total = term if total is None else total + term
    return total


def both(fn, pair):
    return tuple(fn(x) for x in pair)


def kernel(
    n_dp, n_ctx, order_hbm, doc_hbm, q_hbm, k_hbm, v_hbm, d_hbm, g_hbm,
    out_ref, dq_ref, dk_ref, dv_ref, dd_ref,
    order_ref, doc_ref, q_ref, k_ref, v_ref, d_ref, g_ref, in_sem, decay, grow, end, near, dv_near, dq_near, dk_near,
    sx, rx, sy, ry, loc, into, mate_out, mate_in, chain_out, relay_out, chain_in, hop_out, hop_in, before, doc_prev, doc_next,
    x_send, x_recv, y_send, y_recv, mate_send, mate_recv, chain_send, chain_recv, hop_send, hop_recv, far_send, far_recv,
    doc_send, doc_recv,
):
    me = lax.axis_index("dp")
    pos = lax.axis_index("ctx")
    rows = q_hbm.shape[1]
    pairs = q_hbm.shape[2] // KW
    blocks = rows // BLK
    per = blocks // n_dp
    part = per * BLK
    chips = n_ctx // 2
    has_prev = pos > 0
    has_next = pos < n_ctx - 1
    core = lax.rem(pos, 2)
    own = 1 - core
    mate_pos = pos + 1 - 2 * core
    ahead = 4 * core - 2
    chip = pos // 2
    behind = jnp.where(core == 1, chip, chips - 1 - chip)
    second = behind == 1
    third = behind == 2
    spans = spans_of(n_ctx)

    def has_from(span):
        return behind >= span

    def has_to(span):
        return behind + span < chips

    barrier = pltpu.get_barrier_semaphore()
    for r in range(1, n_dp):
        peer = lax.rem(me + r, n_dp)
        pl.semaphore_signal(barrier, inc=1, device_id={"dp": peer}, device_id_type=MESH)

    peers = n_dp - 1
    for step in (-1, 1, *(sign * 2 * span for span in sorted({1, 2, *spans}) for sign in (-1, 1))):
        there = (pos + step >= 0) & (pos + step < n_ctx)
        peers = peers + there.astype(jnp.int32)

        @pl.when(there)
        def _():
            pl.semaphore_signal(barrier, inc=1, device_id={"ctx": pos + step}, device_id_type=MESH)

    fetches = [
        pltpu.make_async_copy(src, dst, in_sem.at[i])
        for i, (src, dst) in enumerate((
            (order_hbm, order_ref), (q_hbm, q_ref), (k_hbm, k_ref), (d_hbm, d_ref),
            (v_hbm, v_ref), (doc_hbm, doc_ref), (g_hbm, g_ref),
        ))
    ]
    for fetch in fetches:
        fetch.start()

    def my_rows(index):
        return pl.ds(pl.multiple_of(index * part, part), part)

    def lanes(h, width):
        return pl.ds(pl.multiple_of(h * width, width), width)

    for fetch in fetches:
        fetch.wait()

    @pl.when(jnp.logical_not(has_prev))
    def _():
        doc_prev[...] = jnp.full_like(doc_prev, -1)

    @pl.when(jnp.logical_not(has_next))
    def _():
        doc_next[...] = jnp.full_like(doc_next, -1)

    for span in (1, 2):
        @pl.when(jnp.logical_not(has_from(span)))
        def _():
            chain_in[span - 1] = jnp.zeros_like(chain_in[span - 1])

    @pl.when(third)
    def _():
        chain_in[1] = jnp.zeros_like(chain_in[1])

    for i, span in enumerate(spans):
        @pl.when(jnp.logical_not(has_from(span)))
        def _():
            hop_in[i] = jnp.zeros_like(hop_in[i])

    order = [order_ref[me, 0, j] for j in range(blocks)]

    def piece(j):
        return slice(j * BLK, (j + 1) * BLK)

    def stage(h, carry):
        for src, width, at in ((q_ref, KW, 0), (k_ref, KW, KW), (d_ref, KW, 2 * KW), (v_ref, VW, 3 * KW)):
            parts = [src[0, piece(j), lanes(h, width)] for j in range(blocks)]
            for dest in range(blocks):
                chosen = parts[0]
                for j in range(1, blocks):
                    chosen = lax.select(order[j] == dest, parts[j], chosen)
                sx[h, piece(dest), at : at + width] = chosen
        return carry

    lax.fori_loop(0, pairs, stage, 0)

    pl.semaphore_wait(barrier, peers)

    def exchange(src, dst, send, recv, h, r):
        peer = lax.rem(me + r, n_dp)
        return pltpu.make_async_remote_copy(
            src_ref=src.at[h, my_rows(peer), :],
            dst_ref=dst.at[h, my_rows(me), :],
            send_sem=send.at[h, r],
            recv_sem=recv.at[h, r],
            device_id={"dp": peer},
            device_id_type=MESH,
        )

    def arrival(src, dst, send, recv, h, r):
        source = lax.rem(me + n_dp - r, n_dp)
        return pltpu.make_async_remote_copy(
            src_ref=src.at[h, my_rows(source), :],
            dst_ref=dst.at[h, my_rows(source), :],
            send_sem=send.at[h, r],
            recv_sem=recv.at[h, r],
            device_id={"dp": source},
            device_id_type=MESH,
        )

    def to_ctx(src, dst, send, recv, there):
        return pltpu.make_async_remote_copy(
            src_ref=src, dst_ref=dst, send_sem=send, recv_sem=recv,
            device_id={"ctx": there}, device_id_type=MESH,
        )

    def doc_up():
        return to_ctx(doc_ref, doc_prev, doc_send.at[0], doc_recv.at[0], pos + 1)

    def doc_down():
        return to_ctx(doc_ref, doc_next, doc_send.at[1], doc_recv.at[1], pos - 1)

    def mate(h):
        return to_ctx(mate_out.at[h], mate_in.at[h], mate_send.at[h], mate_recv.at[h], mate_pos)

    def chain(h, span):
        size = KW + TILE if span == 1 or spans else KW
        return to_ctx(
            chain_out.at[h, 0:size], chain_in.at[span - 1, h, 0:size],
            chain_send.at[h, span - 1], chain_recv.at[h, span - 1], pos + ahead * span,
        )

    def relay(h):
        return to_ctx(
            relay_out.at[h], chain_in.at[0, h], chain_send.at[h, 0], chain_recv.at[h, 0], pos + ahead,
        )

    sends_near = has_to(1) & jnp.logical_not(second)
    sends_far = has_to(2) & (behind > 0)
    relays = has_to(1) & second

    def hop(h, i):
        return to_ctx(hop_out.at[i, h], hop_in.at[i, h], hop_send.at[h, i], hop_recv.at[h, i], pos + ahead * spans[i])

    def far(h):
        return to_ctx(before.at[h], into.at[own, h], far_send.at[h], far_recv.at[h], mate_pos)

    def far_arrival(h):
        return to_ctx(before.at[h], into.at[1 - own, h], far_send.at[h], far_recv.at[h], mate_pos)

    def launch(h, carry):
        for r in range(1, n_dp):
            exchange(sx, rx, x_send, x_recv, h, r).start()
        rx[h, my_rows(me), :] = sx[h, my_rows(me), :]
        return carry

    launch(0, 0)

    @pl.when(has_next)
    def _():
        doc_up().start()

    @pl.when(has_prev)
    def _():
        doc_down().start()

    lax.fori_loop(1, pairs, launch, 0)

    @pl.when(has_prev)
    def _():
        doc_up().wait_recv()

    @pl.when(has_next)
    def _():
        doc_down().wait_recv()

    doc_row = jnp.broadcast_to(doc_ref[...].astype(F32), (rows, rows))
    doc_col = doc_row.T
    first_row = doc_col[0:1, :]
    last_row = doc_col[rows - 1 : rows, :]
    prev_last = jnp.broadcast_to(doc_prev[:, rows - 1 : rows].astype(F32), (1, rows))
    next_first = jnp.broadcast_to(doc_next[:, 0:1].astype(F32), (1, rows))
    use_state = (prev_last == first_row).astype(F32)
    use_carry = (next_first == last_row).astype(F32)
    single = (first_row == last_row).astype(F32)
    pass_state = single * use_state
    pass_carry = single * use_carry
    pass_own = jnp.where(core == 1, pass_state, pass_carry)
    pass_mate = jnp.where(core == 1, pass_carry, pass_state)
    in_first = (doc_col == first_row).astype(F32)
    in_last = (doc_col == last_row).astype(F32)
    head_w = in_first * use_state
    tail_w = in_last * use_carry
    row_id = lax.broadcasted_iota(jnp.int32, (rows, rows), 0)
    lane_id = lax.broadcasted_iota(jnp.int32, (rows, rows), 1)
    same = (doc_row == doc_col) & (row_id >= lane_id)
    later = ((doc_row == doc_col) & (row_id <= lane_id)).astype(BF16)
    lower = (row_id >= lane_id).astype(BF16)
    in_a = lax.broadcasted_iota(jnp.int32, (rows, KW), 1) < DK
    factor = DK ** (-0.5)

    def load(h):
        q = rx[h, :, 0:KW]
        k = rx[h, :, KW : 2 * KW]
        d = rx[h, :, 2 * KW : 3 * KW]
        v = rx[h, :, 3 * KW : W]
        g = g_ref[0, :, lanes(h, VW)]
        cum = dot(lower, d, NN)
        total = cum[rows - 1 : rows, :]
        growth = jnp.exp(cum)
        shrink = jnp.exp(-cum)
        to_end = jnp.exp(total - cum)
        grow[h] = growth
        end[h] = to_end
        return q.astype(F32), k.astype(F32), v, g, d, growth, shrink, to_end, jnp.exp(total)

    def fold(wide):
        return jnp.concatenate([wide[0:DK, 0:DV], wide[DK:KW, DV:VW]], axis=0)

    def spread(tall):
        nil = jnp.zeros((DK, DV), tall.dtype)
        top = jnp.concatenate([tall[0:DK], nil], axis=1)
        low = jnp.concatenate([nil, tall[DK:KW]], axis=1)
        return jnp.concatenate([top, low], axis=0)

    def nearby(h):
        for r in range(1, n_dp):
            arrival(sx, rx, x_send, x_recv, h, r).wait_recv()
        q_f, k_f, v, g, d, growth, shrink, to_end, fade = load(h)
        loc[0, h] = fold(dot(split(k_f * to_end * in_last), v, TN))
        loc[1, h] = factor * fold(dot(split(q_f * growth * in_first), g, TN))
        decay[h] = jnp.exp(dot(d, jnp.ones((rows, DV), BF16), TN))
        mate_out[h, 0:KW] = loc[1 - own, h]
        mate_out[h, KW : 2 * KW] = pass_mate * decay[h]
        mate_out[h, 2 * KW : 2 * KW + TILE] = jnp.broadcast_to(pass_mate * fade, (TILE, KW))
        chain_out[h, KW : KW + TILE] = jnp.broadcast_to(pass_own * fade, (TILE, KW))
        mate(h).start()
        q_t = q_f * growth
        k_t = k_f * shrink
        zero = jnp.zeros_like(q_t)
        q_2 = split(jnp.concatenate([jnp.where(in_a, q_t, zero), jnp.where(in_a, zero, q_t)], axis=0))
        k_s = split(k_t)
        k_2 = split(jnp.concatenate([jnp.where(in_a, k_t, zero), jnp.where(in_a, zero, k_t)], axis=0))
        same_2 = jnp.concatenate([same, same], axis=0)
        score_2 = split(jnp.where(same_2, dot(q_2, k_s, NT), 0.0))
        v_a, v_b = v[:, 0:DV], v[:, DV:VW]
        g_a, g_b = g[:, 0:DV], g[:, DV:VW]
        score_a = both(lambda x: x[0:rows], score_2)
        score_b = both(lambda x: x[rows : 2 * rows], score_2)
        near[h, :, 0:DV] = dot(score_a, v_a, NN)
        near[h, :, DV:VW] = dot(score_b, v_b, NN)
        dv_near[h, :, 0:DV] = dot(score_a, g_a, TN)
        dv_near[h, :, DV:VW] = dot(score_b, g_b, TN)
        gs_a = jnp.where(same, dot(g_a, v_a, NT), 0.0)
        gs_b = jnp.where(same, dot(g_b, v_b, NT), 0.0)
        dq_near[h] = dot(split(jnp.concatenate([gs_a, gs_b], axis=1)), k_2, NN)
        dk_near[h] = factor * shrink * dot(split(jnp.concatenate([gs_a, gs_b], axis=0)), q_2, TN)

    def finish(h):
        far_arrival(h).wait_recv()
        q_f = rx[h, :, 0:KW].astype(F32)
        k_f = rx[h, :, KW : 2 * KW].astype(F32)
        v = rx[h, :, 3 * KW : W]
        g = g_ref[0, :, lanes(h, VW)]
        growth = grow[h]
        to_end = end[h]
        q_t = q_f * growth
        k_e = k_f * to_end * tail_w
        f_in = into[0, h]
        b_in = into[1, h]
        f_end = loc[0, h] + pass_state * decay[h] * f_in
        state = both(spread, split(f_in))
        carry = both(spread, split(b_in))
        far = dot(split(q_t * head_w), state, NN)
        out_ref[0, :, lanes(h, VW)] = (factor * (near[h] + far)).astype(BF16)
        dq = factor * growth * (dq_near[h] + dot(g, state, NT) * head_w)
        dk = dk_near[h] + to_end * dot(v, carry, NT) * tail_w
        dv = factor * dv_near[h] + dot(split(k_e), carry, NN)
        log_grad = q_f * dq - k_f * dk
        sums = dot(jnp.ones((8, DV), BF16), split(f_end * b_in), NT)
        dd = dot(later, split(log_grad), NN) + sums[0:1] * tail_w
        sy[h, :, 0:KW] = dq.astype(BF16)
        sy[h, :, KW : 2 * KW] = dk.astype(BF16)
        sy[h, :, 2 * KW : 3 * KW] = dd.astype(BF16)
        sy[h, :, 3 * KW : W] = dv.astype(BF16)
        ry[h, my_rows(me), :] = sy[h, my_rows(me), :]
        for r in range(1, n_dp):
            exchange(sy, ry, y_send, y_recv, h, r).start()

    def column(tile):
        return jnp.broadcast_to(tile[0:1], (DV, KW)).T

    def depart(h):
        mate(h).wait_recv()
        chain_out[h, 0:KW] = loc[own, h] + pass_own * decay[h] * mate_in[h, 0:KW]
        chain_out[h, KW : KW + TILE] = chain_out[h, KW : KW + TILE] * mate_in[h, 2 * KW : 2 * KW + TILE]

        @pl.when(sends_near)
        def _():
            chain(h, 1).start()

        @pl.when(sends_far)
        def _():
            chain(h, 2).start()

    def join(h, near_ref, far_ref, i):
        fade = near_ref[KW : KW + TILE]
        state = near_ref[0:KW] + column(fade) * far_ref[0:KW]
        if i < len(spans):
            hop_out[i, h, 0:KW] = state
            hop_out[i, h, KW : KW + TILE] = fade * far_ref[KW : KW + TILE]

            @pl.when(has_to(spans[i]))
            def _():
                hop(h, i).start()
        else:
            before[h] = state
            far(h).start()
            into[own, h] = mate_in[h, 0:KW] + mate_in[h, KW : 2 * KW] * state

    def arrive(h):
        @pl.when(has_from(1))
        def _():
            chain(h, 1).wait_recv()

        @pl.when(has_from(3))
        def _():
            chain(h, 2).wait_recv()

        @pl.when(relays)
        def _():
            fade = chain_out[h, KW : KW + TILE]
            relay_out[h, 0:KW] = chain_out[h, 0:KW] + column(fade) * chain_in[0, h, 0:KW]
            relay_out[h, KW : KW + TILE] = fade
            relay(h).start()

        join(h, chain_in.at[0, h], chain_in.at[1, h], 0)

    def widen(h, i):
        @pl.when(has_from(spans[i]))
        def _():
            hop(h, i).wait_recv()
        join(h, hop_out.at[i, h], hop_in.at[i, h], i + 1)

    def flight(place):
        return jnp.where(place == 2, 2 * FLIGHT, jnp.where(place > 2, FAR_FLIGHT, FLIGHT))

    stages = [(0, nearby), (flight(behind), arrive), (0, depart)]
    last = max(2 * FLIGHT, FAR_FLIGHT) + 1
    for i in range(len(spans)):
        stages.append((last + i * FAR_FLIGHT, functools.partial(widen, i=i)))
    if spans:
        last += len(spans) * FAR_FLIGHT
        stages.insert(1, (last, finish))
    else:
        stages.insert(1, (jnp.maximum(flight(behind), flight(chips - 1 - behind)) + 1, finish))

    def step(t, carry):
        for lag, stage_of in stages:
            @pl.when((t >= lag) & (t < lag + pairs))
            def _():
                stage_of(t - lag)

        return carry

    lax.fori_loop(0, last + pairs, step, 0)

    @pl.when(has_next)
    def _():
        doc_up().wait_send()

    @pl.when(has_prev)
    def _():
        doc_down().wait_send()

    def home(h, carry):
        mate(h).wait_send()
        far(h).wait_send()

        @pl.when(has_to(1))
        def _():
            chain(h, 1).wait_send()

        @pl.when(sends_far)
        def _():
            chain(h, 2).wait_send()

        for i, span in enumerate(spans):
            @pl.when(has_to(span))
            def _():
                hop(h, i).wait_send()
        for r in range(1, n_dp):
            exchange(sx, rx, x_send, x_recv, h, r).wait_send()
            exchange(sy, ry, y_send, y_recv, h, r).wait_send()
        for r in range(1, n_dp):
            arrival(sy, ry, y_send, y_recv, h, r).wait_recv()
        for dst, width, at in ((dq_ref, KW, 0), (dk_ref, KW, KW), (dd_ref, KW, 2 * KW), (dv_ref, VW, 3 * KW)):
            parts = [ry[h, piece(j), at : at + width] for j in range(blocks)]
            for j in range(blocks):
                chosen = parts[0]
                for source in range(1, blocks):
                    chosen = lax.select(order[j] == source, parts[source], chosen)
                dst[0, piece(j), lanes(h, width)] = chosen
        return carry

    lax.fori_loop(0, pairs, home, 0)


def store(*refs):
    half = len(refs) // 2
    sem = refs[-1]
    copies = [pltpu.make_async_copy(refs[i], refs[half + i], sem.at[i]) for i in range(half)]
    for copy in copies:
        copy.start()
    for copy in copies:
        copy.wait()


def spans_of(n_ctx):
    chips = n_ctx // 2
    span, spans = 2, []
    while span < chips // 2:
        spans.append(span)
        span *= 2
    return spans


def body(n_dp, n_ctx, query_rows, key_rows, value_rows, log_decay, out_grad, doc_ids, block_order):
    rows, hk = query_rows.shape[1:]
    hv = value_rows.shape[2]
    pairs = hk // KW
    rounds = max(len(spans_of(n_ctx)), 1)
    vmem = pl.BlockSpec(memory_space=pltpu.VMEM)
    keys = jax.ShapeDtypeStruct((1, rows, hk), BF16)
    values = jax.ShapeDtypeStruct((1, rows, hv), BF16)
    outs = (values, keys, keys, values, keys)
    dma = pltpu.SemaphoreType.DMA
    held = pl.pallas_call(
        functools.partial(kernel, n_dp, n_ctx),
        out_shape=tuple(pltpu.VMEM(x.shape, BF16) for x in outs),
        in_specs=[pl.BlockSpec(memory_space=pltpu.HBM)] * 7,
        out_specs=(vmem,) * 5,
        scratch_shapes=[
            pltpu.SMEM(block_order.shape, jnp.int32),
            pltpu.VMEM((1, rows), jnp.int32),
            pltpu.VMEM((1, rows, hk), BF16),
            pltpu.VMEM((1, rows, hk), BF16),
            pltpu.VMEM((1, rows, hv), BF16),
            pltpu.VMEM((1, rows, hk), BF16),
            pltpu.VMEM((1, rows, hv), BF16),
            dma((7,)),
            pltpu.VMEM((pairs, KW, DV), F32),
            pltpu.VMEM((pairs, rows, KW), F32),
            pltpu.VMEM((pairs, rows, KW), F32),
            pltpu.VMEM((pairs, rows, VW), F32),
            pltpu.VMEM((pairs, rows, VW), F32),
            pltpu.VMEM((pairs, rows, KW), F32),
            pltpu.VMEM((pairs, rows, KW), F32),
            pltpu.VMEM((pairs, rows, W), BF16),
            pltpu.VMEM((pairs, rows, W), BF16),
            pltpu.VMEM((pairs, rows, W), BF16),
            pltpu.VMEM((pairs, rows, W), BF16),
            pltpu.VMEM((2, pairs, KW, DV), F32),
            pltpu.VMEM((2, pairs, KW, DV), F32),
            pltpu.VMEM((pairs, 2 * KW + TILE, DV), F32),
            pltpu.VMEM((pairs, 2 * KW + TILE, DV), F32),
            pltpu.VMEM((pairs, KW + TILE, DV), F32),
            pltpu.VMEM((pairs, KW + TILE, DV), F32),
            pltpu.VMEM((2, pairs, KW + TILE, DV), F32),
            pltpu.VMEM((rounds, pairs, KW + TILE, DV), F32),
            pltpu.VMEM((rounds, pairs, KW + TILE, DV), F32),
            pltpu.VMEM((pairs, KW, DV), F32),
            pltpu.VMEM((1, rows), jnp.int32),
            pltpu.VMEM((1, rows), jnp.int32),
            dma((pairs, n_dp)), dma((pairs, n_dp)), dma((pairs, n_dp)), dma((pairs, n_dp)),
            dma((pairs,)), dma((pairs,)), dma((pairs, 2)), dma((pairs, 2)), dma((pairs, rounds)), dma((pairs, rounds)),
            dma((pairs,)), dma((pairs,)),
            dma((2,)), dma((2,)),
        ],
        compiler_params=pltpu.CompilerParams(
            collective_id=0, has_side_effects=True, vmem_limit_bytes=56 * 1024 * 1024
        ),
    )(block_order, doc_ids, query_rows, key_rows, value_rows, log_decay, out_grad)
    return pl.pallas_call(
        store,
        out_shape=outs,
        in_specs=(vmem,) * 5,
        out_specs=(pl.BlockSpec(memory_space=pltpu.HBM),) * 5,
        scratch_shapes=[dma((5,))],
    )(*(pltpu.with_memory_space_constraint(x, pltpu.VMEM) for x in held))


def solution(mesh):
    placed = P("dp", "ctx", None)
    return jax.shard_map(
        functools.partial(body, mesh.shape["dp"], mesh.shape["ctx"]),
        mesh=mesh,
        in_specs=(placed,) * 5 + (P("dp", "ctx"), P(None, "ctx", None)),
        out_specs=(placed,) * 5,
        check_vma=False,
    )
```

```python
import functools

import jax
import jax.numpy as jnp
from jax import lax
from jax.experimental import pallas as pl
from jax.experimental.pallas import tpu as pltpu
from jax.sharding import PartitionSpec as P

DK = 64
DV = 128
BLK = 32
KW = 2 * DK
VW = 2 * DV
W = 3 * KW + VW
TILE = 8
FLIGHT = 2
FAR_FLIGHT = 3
MESH = pl.DeviceIdType.MESH
F32 = jnp.float32
BF16 = jnp.bfloat16

NN = (((1,), (0,)), ((), ()))
NT = (((1,), (1,)), ((), ()))
TN = (((0,), (0,)), ((), ()))


def split(x):
    hi = x.astype(BF16)
    return hi, (x - hi.astype(F32)).astype(BF16)


def dot(a, b, dims):
    a = a if isinstance(a, tuple) else (a,)
    b = b if isinstance(b, tuple) else (b,)
    total = None
    for i, left in enumerate(a):
        for j, right in enumerate(b):
            if i + j > 1:
                continue
            term = lax.dot_general(left, right, dims, preferred_element_type=F32)
            total = term if total is None else total + term
    return total


def both(fn, pair):
    return tuple(fn(x) for x in pair)


def kernel(
    n_dp, n_ctx, order_hbm, doc_hbm, q_hbm, k_hbm, v_hbm, d_hbm, g_hbm,
    out_ref, dq_ref, dk_ref, dv_ref, dd_ref,
    order_ref, doc_ref, q_ref, k_ref, v_ref, d_ref, g_ref, in_sem, decay, grow, end, near, dv_near, dq_near, dk_near,
    sx, rx, sy, ry, loc, into, mate_out, mate_in, chain_out, relay_out, chain_in, hop_out, hop_in, before, doc_prev, doc_next,
    x_send, x_recv, y_send, y_recv, mate_send, mate_recv, chain_send, chain_recv, hop_send, hop_recv, far_send, far_recv,
    doc_send, doc_recv,
):
    me = lax.axis_index("dp")
    pos = lax.axis_index("ctx")
    rows = q_hbm.shape[1]
    pairs = q_hbm.shape[2] // KW
    blocks = rows // BLK
    per = blocks // n_dp
    part = per * BLK
    chips = n_ctx // 2
    has_prev = pos > 0
    has_next = pos < n_ctx - 1
    core = lax.rem(pos, 2)
    own = 1 - core
    mate_pos = pos + 1 - 2 * core
    ahead = 4 * core - 2
    chip = pos // 2
    behind = jnp.where(core == 1, chip, chips - 1 - chip)
    second = behind == 1
    third = behind == 2
    spans = spans_of(n_ctx)

    def has_from(span):
        return behind >= span

    def has_to(span):
        return behind + span < chips

    barrier = pltpu.get_barrier_semaphore()
    for r in range(1, n_dp):
        peer = lax.rem(me + r, n_dp)
        pl.semaphore_signal(barrier, inc=1, device_id={"dp": peer}, device_id_type=MESH)

    peers = n_dp - 1
    for step in (-1, 1, *(sign * 2 * span for span in sorted({1, 2, *spans}) for sign in (-1, 1))):
        there = (pos + step >= 0) & (pos + step < n_ctx)
        peers = peers + there.astype(jnp.int32)

        @pl.when(there)
        def _():
            pl.semaphore_signal(barrier, inc=1, device_id={"ctx": pos + step}, device_id_type=MESH)

    fetches = [
        pltpu.make_async_copy(src, dst, in_sem.at[i])
        for i, (src, dst) in enumerate((
            (order_hbm, order_ref), (q_hbm, q_ref), (k_hbm, k_ref), (d_hbm, d_ref),
            (v_hbm, v_ref), (doc_hbm, doc_ref), (g_hbm, g_ref),
        ))
    ]
    for fetch in fetches:
        fetch.start()

    def my_rows(index):
        return pl.ds(pl.multiple_of(index * part, part), part)

    def lanes(h, width):
        return pl.ds(pl.multiple_of(h * width, width), width)

    for fetch in fetches:
        fetch.wait()

    @pl.when(jnp.logical_not(has_prev))
    def _():
        doc_prev[...] = jnp.full_like(doc_prev, -1)

    @pl.when(jnp.logical_not(has_next))
    def _():
        doc_next[...] = jnp.full_like(doc_next, -1)

    for span in (1, 2):
        @pl.when(jnp.logical_not(has_from(span)))
        def _():
            chain_in[span - 1] = jnp.zeros_like(chain_in[span - 1])

    @pl.when(third)
    def _():
        chain_in[1] = jnp.zeros_like(chain_in[1])

    for i, span in enumerate(spans):
        @pl.when(jnp.logical_not(has_from(span)))
        def _():
            hop_in[i] = jnp.zeros_like(hop_in[i])

    order = [order_ref[me, 0, j] for j in range(blocks)]

    def piece(j):
        return slice(j * BLK, (j + 1) * BLK)

    def stage(h, carry):
        for src, width, at in ((q_ref, KW, 0), (k_ref, KW, KW), (d_ref, KW, 2 * KW), (v_ref, VW, 3 * KW)):
            parts = [src[0, piece(j), lanes(h, width)] for j in range(blocks)]
            for dest in range(blocks):
                chosen = parts[0]
                for j in range(1, blocks):
                    chosen = lax.select(order[j] == dest, parts[j], chosen)
                sx[h, piece(dest), at : at + width] = chosen
        return carry

    lax.fori_loop(0, pairs, stage, 0)

    pl.semaphore_wait(barrier, peers)

    def exchange(src, dst, send, recv, h, r):
        peer = lax.rem(me + r, n_dp)
        return pltpu.make_async_remote_copy(
            src_ref=src.at[h, my_rows(peer), :],
            dst_ref=dst.at[h, my_rows(me), :],
            send_sem=send.at[h, r],
            recv_sem=recv.at[h, r],
            device_id={"dp": peer},
            device_id_type=MESH,
        )

    def arrival(src, dst, send, recv, h, r):
        source = lax.rem(me + n_dp - r, n_dp)
        return pltpu.make_async_remote_copy(
            src_ref=src.at[h, my_rows(source), :],
            dst_ref=dst.at[h, my_rows(source), :],
            send_sem=send.at[h, r],
            recv_sem=recv.at[h, r],
            device_id={"dp": source},
            device_id_type=MESH,
        )

    def to_ctx(src, dst, send, recv, there):
        return pltpu.make_async_remote_copy(
            src_ref=src, dst_ref=dst, send_sem=send, recv_sem=recv,
            device_id={"ctx": there}, device_id_type=MESH,
        )

    def doc_up():
        return to_ctx(doc_ref, doc_prev, doc_send.at[0], doc_recv.at[0], pos + 1)

    def doc_down():
        return to_ctx(doc_ref, doc_next, doc_send.at[1], doc_recv.at[1], pos - 1)

    def mate(h):
        return to_ctx(mate_out.at[h], mate_in.at[h], mate_send.at[h], mate_recv.at[h], mate_pos)

    def chain(h, span):
        size = KW + TILE if span == 1 or spans else KW
        return to_ctx(
            chain_out.at[h, 0:size], chain_in.at[span - 1, h, 0:size],
            chain_send.at[h, span - 1], chain_recv.at[h, span - 1], pos + ahead * span,
        )

    def relay(h):
        return to_ctx(
            relay_out.at[h], chain_in.at[0, h], chain_send.at[h, 0], chain_recv.at[h, 0], pos + ahead,
        )

    sends_near = has_to(1) & jnp.logical_not(second)
    sends_far = has_to(2) & (behind > 0)
    relays = has_to(1) & second

    def hop(h, i):
        return to_ctx(hop_out.at[i, h], hop_in.at[i, h], hop_send.at[h, i], hop_recv.at[h, i], pos + ahead * spans[i])

    def far(h):
        return to_ctx(before.at[h], into.at[own, h], far_send.at[h], far_recv.at[h], mate_pos)

    def far_arrival(h):
        return to_ctx(before.at[h], into.at[1 - own, h], far_send.at[h], far_recv.at[h], mate_pos)

    def launch(h, carry):
        for r in range(1, n_dp):
            exchange(sx, rx, x_send, x_recv, h, r).start()
        return carry

    launch(0, 0)

    @pl.when(has_next)
    def _():
        doc_up().start()

    @pl.when(has_prev)
    def _():
        doc_down().start()

    lax.fori_loop(1, pairs, launch, 0)

    @pl.when(has_prev)
    def _():
        doc_up().wait_recv()

    @pl.when(has_next)
    def _():
        doc_down().wait_recv()

    doc_row = jnp.broadcast_to(doc_ref[...].astype(F32), (rows, rows))
    doc_col = doc_row.T
    first_row = doc_col[0:1, :]
    last_row = doc_col[rows - 1 : rows, :]
    prev_last = jnp.broadcast_to(doc_prev[:, rows - 1 : rows].astype(F32), (1, rows))
    next_first = jnp.broadcast_to(doc_next[:, 0:1].astype(F32), (1, rows))
    use_state = (prev_last == first_row).astype(F32)
    use_carry = (next_first == last_row).astype(F32)
    single = (first_row == last_row).astype(F32)
    pass_state = single * use_state
    pass_carry = single * use_carry
    pass_own = jnp.where(core == 1, pass_state, pass_carry)
    pass_mate = jnp.where(core == 1, pass_carry, pass_state)
    in_first = (doc_col == first_row).astype(F32)
    in_last = (doc_col == last_row).astype(F32)
    head_w = in_first * use_state
    tail_w = in_last * use_carry
    row_id = lax.broadcasted_iota(jnp.int32, (rows, rows), 0)
    lane_id = lax.broadcasted_iota(jnp.int32, (rows, rows), 1)
    same = (doc_row == doc_col) & (row_id >= lane_id)
    later = ((doc_row == doc_col) & (row_id <= lane_id)).astype(BF16)
    lower = (row_id >= lane_id).astype(BF16)
    in_a = lax.broadcasted_iota(jnp.int32, (rows, KW), 1) < DK
    factor = DK ** (-0.5)

    def load(h):
        q = rx[h, :, 0:KW]
        k = rx[h, :, KW : 2 * KW]
        d = rx[h, :, 2 * KW : 3 * KW]
        v = rx[h, :, 3 * KW : W]
        g = g_ref[0, :, lanes(h, VW)]
        cum = dot(lower, d, NN)
        total = cum[rows - 1 : rows, :]
        growth = jnp.exp(cum)
        shrink = jnp.exp(-cum)
        to_end = jnp.exp(total - cum)
        grow[h] = growth
        end[h] = to_end
        return q.astype(F32), k.astype(F32), v, g, d, growth, shrink, to_end, jnp.exp(total)

    def fold(wide):
        return jnp.concatenate([wide[0:DK, 0:DV], wide[DK:KW, DV:VW]], axis=0)

    def spread(tall):
        nil = jnp.zeros((DK, DV), tall.dtype)
        top = jnp.concatenate([tall[0:DK], nil], axis=1)
        low = jnp.concatenate([nil, tall[DK:KW]], axis=1)
        return jnp.concatenate([top, low], axis=0)

    def nearby(h):
        rx[h, my_rows(me), :] = sx[h, my_rows(me), :]
        for r in range(1, n_dp):
            arrival(sx, rx, x_send, x_recv, h, r).wait_recv()
        q_f, k_f, v, g, d, growth, shrink, to_end, fade = load(h)
        loc[0, h] = fold(dot(split(k_f * to_end * in_last), v, TN))
        loc[1, h] = factor * fold(dot(split(q_f * growth * in_first), g, TN))
        decay[h] = jnp.exp(dot(d, jnp.ones((rows, DV), BF16), TN))
        mate_out[h, 0:KW] = loc[1 - own, h]
        mate_out[h, KW : 2 * KW] = pass_mate * decay[h]
        mate_out[h, 2 * KW : 2 * KW + TILE] = jnp.broadcast_to(pass_mate * fade, (TILE, KW))
        chain_out[h, KW : KW + TILE] = jnp.broadcast_to(pass_own * fade, (TILE, KW))
        mate(h).start()
        q_t = q_f * growth
        k_t = k_f * shrink
        zero = jnp.zeros_like(q_t)
        q_2 = split(jnp.concatenate([jnp.where(in_a, q_t, zero), jnp.where(in_a, zero, q_t)], axis=0))
        k_s = split(k_t)
        k_2 = split(jnp.concatenate([jnp.where(in_a, k_t, zero), jnp.where(in_a, zero, k_t)], axis=0))
        same_2 = jnp.concatenate([same, same], axis=0)
        score_2 = split(jnp.where(same_2, dot(q_2, k_s, NT), 0.0))
        v_a, v_b = v[:, 0:DV], v[:, DV:VW]
        g_a, g_b = g[:, 0:DV], g[:, DV:VW]
        score_a = both(lambda x: x[0:rows], score_2)
        score_b = both(lambda x: x[rows : 2 * rows], score_2)
        near[h, :, 0:DV] = dot(score_a, v_a, NN)
        near[h, :, DV:VW] = dot(score_b, v_b, NN)
        dv_near[h, :, 0:DV] = dot(score_a, g_a, TN)
        dv_near[h, :, DV:VW] = dot(score_b, g_b, TN)
        gs_a = jnp.where(same, dot(g_a, v_a, NT), 0.0)
        gs_b = jnp.where(same, dot(g_b, v_b, NT), 0.0)
        dq_near[h] = dot(split(jnp.concatenate([gs_a, gs_b], axis=1)), k_2, NN)
        dk_near[h] = factor * shrink * dot(split(jnp.concatenate([gs_a, gs_b], axis=0)), q_2, TN)

    def finish(h):
        far_arrival(h).wait_recv()
        q_f = rx[h, :, 0:KW].astype(F32)
        k_f = rx[h, :, KW : 2 * KW].astype(F32)
        v = rx[h, :, 3 * KW : W]
        g = g_ref[0, :, lanes(h, VW)]
        growth = grow[h]
        to_end = end[h]
        q_t = q_f * growth
        k_e = k_f * to_end * tail_w
        f_in = into[0, h]
        b_in = into[1, h]
        f_end = loc[0, h] + pass_state * decay[h] * f_in
        state = both(spread, split(f_in))
        carry = both(spread, split(b_in))
        far = dot(split(q_t * head_w), state, NN)
        out_ref[0, :, lanes(h, VW)] = (factor * (near[h] + far)).astype(BF16)
        dq = factor * growth * (dq_near[h] + dot(g, state, NT) * head_w)
        dk = dk_near[h] + to_end * dot(v, carry, NT) * tail_w
        dv = factor * dv_near[h] + dot(split(k_e), carry, NN)
        log_grad = q_f * dq - k_f * dk
        sums = dot(jnp.ones((8, DV), BF16), split(f_end * b_in), NT)
        dd = dot(later, split(log_grad), NN) + sums[0:1] * tail_w
        sy[h, :, 0:KW] = dq.astype(BF16)
        sy[h, :, KW : 2 * KW] = dk.astype(BF16)
        sy[h, :, 2 * KW : 3 * KW] = dd.astype(BF16)
        sy[h, :, 3 * KW : W] = dv.astype(BF16)
        ry[h, my_rows(me), :] = sy[h, my_rows(me), :]
        for r in range(1, n_dp):
            exchange(sy, ry, y_send, y_recv, h, r).start()

    def column(tile):
        return jnp.broadcast_to(tile[0:1], (DV, KW)).T

    def depart(h):
        mate(h).wait_recv()
        chain_out[h, 0:KW] = loc[own, h] + pass_own * decay[h] * mate_in[h, 0:KW]
        chain_out[h, KW : KW + TILE] = chain_out[h, KW : KW + TILE] * mate_in[h, 2 * KW : 2 * KW + TILE]

        @pl.when(sends_near)
        def _():
            chain(h, 1).start()

        @pl.when(sends_far)
        def _():
            chain(h, 2).start()

    def join(h, near_ref, far_ref, i):
        fade = near_ref[KW : KW + TILE]
        state = near_ref[0:KW] + column(fade) * far_ref[0:KW]
        if i < len(spans):
            hop_out[i, h, 0:KW] = state
            hop_out[i, h, KW : KW + TILE] = fade * far_ref[KW : KW + TILE]

            @pl.when(has_to(spans[i]))
            def _():
                hop(h, i).start()
        else:
            before[h] = state
            far(h).start()
            into[own, h] = mate_in[h, 0:KW] + mate_in[h, KW : 2 * KW] * state

    def arrive(h):
        @pl.when(has_from(1))
        def _():
            chain(h, 1).wait_recv()

        @pl.when(has_from(3))
        def _():
            chain(h, 2).wait_recv()

        @pl.when(relays)
        def _():
            fade = chain_out[h, KW : KW + TILE]
            relay_out[h, 0:KW] = chain_out[h, 0:KW] + column(fade) * chain_in[0, h, 0:KW]
            relay_out[h, KW : KW + TILE] = fade
            relay(h).start()

        join(h, chain_in.at[0, h], chain_in.at[1, h], 0)

    def widen(h, i):
        @pl.when(has_from(spans[i]))
        def _():
            hop(h, i).wait_recv()
        join(h, hop_out.at[i, h], hop_in.at[i, h], i + 1)

    def flight(place):
        return jnp.where(place == 2, 2 * FLIGHT, jnp.where(place > 2, FAR_FLIGHT, FLIGHT))

    stages = [(0, nearby), (flight(behind), arrive), (0, depart)]
    last = max(2 * FLIGHT, FAR_FLIGHT) + 1
    for i in range(len(spans)):
        stages.append((last + i * FAR_FLIGHT, functools.partial(widen, i=i)))
    if spans:
        last += len(spans) * FAR_FLIGHT
        stages.insert(1, (last, finish))
    else:
        stages.insert(1, (jnp.maximum(flight(behind), flight(chips - 1 - behind)) + 1, finish))

    def step(t, carry):
        for lag, stage_of in stages:
            @pl.when((t >= lag) & (t < lag + pairs))
            def _():
                stage_of(t - lag)

        return carry

    lax.fori_loop(0, last + pairs, step, 0)

    @pl.when(has_next)
    def _():
        doc_up().wait_send()

    @pl.when(has_prev)
    def _():
        doc_down().wait_send()

    def home(h, carry):
        mate(h).wait_send()
        far(h).wait_send()

        @pl.when(has_to(1))
        def _():
            chain(h, 1).wait_send()

        @pl.when(sends_far)
        def _():
            chain(h, 2).wait_send()

        for i, span in enumerate(spans):
            @pl.when(has_to(span))
            def _():
                hop(h, i).wait_send()
        for r in range(1, n_dp):
            exchange(sx, rx, x_send, x_recv, h, r).wait_send()
            exchange(sy, ry, y_send, y_recv, h, r).wait_send()
        for r in range(1, n_dp):
            arrival(sy, ry, y_send, y_recv, h, r).wait_recv()
        for dst, width, at in ((dq_ref, KW, 0), (dk_ref, KW, KW), (dd_ref, KW, 2 * KW), (dv_ref, VW, 3 * KW)):
            parts = [ry[h, piece(j), at : at + width] for j in range(blocks)]
            for j in range(blocks):
                chosen = parts[0]
                for source in range(1, blocks):
                    chosen = lax.select(order[j] == source, parts[source], chosen)
                dst[0, piece(j), lanes(h, width)] = chosen
        return carry

    lax.fori_loop(0, pairs, home, 0)


def store(*refs):
    half = len(refs) // 2
    sem = refs[-1]
    copies = [pltpu.make_async_copy(refs[i], refs[half + i], sem.at[i]) for i in range(half)]
    for copy in copies:
        copy.start()
    for copy in copies:
        copy.wait()


def spans_of(n_ctx):
    chips = n_ctx // 2
    span, spans = 2, []
    while span < chips // 2:
        spans.append(span)
        span *= 2
    return spans


def body(n_dp, n_ctx, query_rows, key_rows, value_rows, log_decay, out_grad, doc_ids, block_order):
    rows, hk = query_rows.shape[1:]
    hv = value_rows.shape[2]
    pairs = hk // KW
    rounds = max(len(spans_of(n_ctx)), 1)
    vmem = pl.BlockSpec(memory_space=pltpu.VMEM)
    keys = jax.ShapeDtypeStruct((1, rows, hk), BF16)
    values = jax.ShapeDtypeStruct((1, rows, hv), BF16)
    outs = (values, keys, keys, values, keys)
    dma = pltpu.SemaphoreType.DMA
    held = pl.pallas_call(
        functools.partial(kernel, n_dp, n_ctx),
        out_shape=tuple(pltpu.VMEM(x.shape, BF16) for x in outs),
        in_specs=[pl.BlockSpec(memory_space=pltpu.HBM)] * 7,
        out_specs=(vmem,) * 5,
        scratch_shapes=[
            pltpu.SMEM(block_order.shape, jnp.int32),
            pltpu.VMEM((1, rows), jnp.int32),
            pltpu.VMEM((1, rows, hk), BF16),
            pltpu.VMEM((1, rows, hk), BF16),
            pltpu.VMEM((1, rows, hv), BF16),
            pltpu.VMEM((1, rows, hk), BF16),
            pltpu.VMEM((1, rows, hv), BF16),
            dma((7,)),
            pltpu.VMEM((pairs, KW, DV), F32),
            pltpu.VMEM((pairs, rows, KW), F32),
            pltpu.VMEM((pairs, rows, KW), F32),
            pltpu.VMEM((pairs, rows, VW), F32),
            pltpu.VMEM((pairs, rows, VW), F32),
            pltpu.VMEM((pairs, rows, KW), F32),
            pltpu.VMEM((pairs, rows, KW), F32),
            pltpu.VMEM((pairs, rows, W), BF16),
            pltpu.VMEM((pairs, rows, W), BF16),
            pltpu.VMEM((pairs, rows, W), BF16),
            pltpu.VMEM((pairs, rows, W), BF16),
            pltpu.VMEM((2, pairs, KW, DV), F32),
            pltpu.VMEM((2, pairs, KW, DV), F32),
            pltpu.VMEM((pairs, 2 * KW + TILE, DV), F32),
            pltpu.VMEM((pairs, 2 * KW + TILE, DV), F32),
            pltpu.VMEM((pairs, KW + TILE, DV), F32),
            pltpu.VMEM((pairs, KW + TILE, DV), F32),
            pltpu.VMEM((2, pairs, KW + TILE, DV), F32),
            pltpu.VMEM((rounds, pairs, KW + TILE, DV), F32),
            pltpu.VMEM((rounds, pairs, KW + TILE, DV), F32),
            pltpu.VMEM((pairs, KW, DV), F32),
            pltpu.VMEM((1, rows), jnp.int32),
            pltpu.VMEM((1, rows), jnp.int32),
            dma((pairs, n_dp)), dma((pairs, n_dp)), dma((pairs, n_dp)), dma((pairs, n_dp)),
            dma((pairs,)), dma((pairs,)), dma((pairs, 2)), dma((pairs, 2)), dma((pairs, rounds)), dma((pairs, rounds)),
            dma((pairs,)), dma((pairs,)),
            dma((2,)), dma((2,)),
        ],
        compiler_params=pltpu.CompilerParams(
            collective_id=0, has_side_effects=True, vmem_limit_bytes=56 * 1024 * 1024
        ),
    )(block_order, doc_ids, query_rows, key_rows, value_rows, log_decay, out_grad)
    return pl.pallas_call(
        store,
        out_shape=outs,
        in_specs=(vmem,) * 5,
        out_specs=(pl.BlockSpec(memory_space=pltpu.HBM),) * 5,
        scratch_shapes=[dma((5,))],
    )(*(pltpu.with_memory_space_constraint(x, pltpu.VMEM) for x in held))


def solution(mesh):
    placed = P("dp", "ctx", None)
    return jax.shard_map(
        functools.partial(body, mesh.shape["dp"], mesh.shape["ctx"]),
        mesh=mesh,
        in_specs=(placed,) * 5 + (P("dp", "ctx"), P(None, "ctx", None)),
        out_specs=(placed,) * 5,
        check_vma=False,
    )
```
